256 devices in a mesh: sky: 32 (over y, z_lo, core), loop: 8 (over x, z_hi).
Axes of the slice: x: 4, y: 4, z: 8 (z_hi: 2, z_lo: 4; z = z_hi * 4 + z_lo), core: 2. Of those that a mesh axis runs over, the one named last changes fastest.
Arguments:
- queries: bfloat16 [196608, 256], P(('sky', 'loop')), may hold values from -1 to 1
- keys: bfloat16 [196608, 256], P(('sky', 'loop')), may hold values from -1 to 1
- partner_owner: int32 [196608, 4], P(('sky', 'loop')), may hold values from 0 to 31, as said below
- partner_row: int32 [196608, 4], P(('sky', 'loop')), may hold values from 0 to 767
- partner_count: int32 [196608], P(('sky', 'loop')), may hold values from 1 to 4, as said below
Outputs:
- loss: float32 [196608], P(('sky', 'loop'))
- grad_queries: float32 [196608, 256], P(('sky', 'loop'))
- grad_keys: float32 [196608, 256], P(('sky', 'loop'))
The draws below stay inside these ranges and needn't reach their ends.
Inputs may be any that keep to these rules, and one draw needn't show every extreme that they name: `partner_owner`: each row names 4 different sky indices, never its own device's sky index; among the rows of one device no index is named more than 192 times, and on every device some index is named exactly 192 times. `partner_count`: some anchor has 4 live partners and some has one.
All inputs are finite; a program needn't handle non-finite values.
Results may differ from the reference program's by a relative error of at most 0.004.
Values may be sent and summed in bfloat16 or wider, within the bound.
A program may use at most 64 MiB of HBM per device.

```python
import jax
import jax.numpy as jnp
from jax import lax

D = 256
ANCHORS = 768
PARTNERS = 4
BUCKET = 192
GROUP = 6144
ROWS = 196608
N_LOOP = 8


def draw_codes(key):
    devices = ROWS // ANCHORS
    subkeys = jax.random.split(jax.random.fold_in(key, 31), devices)
    return jax.vmap(lambda subkey: jax.random.permutation(subkey, ANCHORS))(subkeys).astype(jnp.int32)


def draw_routes(key):
    devices = ROWS // ANCHORS
    sky_count = ROWS // GROUP
    others = sky_count - 1
    couples = (sky_count - 2) // 2
    codes = draw_codes(key)
    device_ids = jnp.arange(devices, dtype=jnp.int32)
    sky_of = device_ids // N_LOOP
    loop_of = device_ids % N_LOOP
    hot = jax.random.randint(jax.random.fold_in(key, 32), (), 0, sky_count, dtype=jnp.int32)
    rank_keys = jax.random.split(jax.random.fold_in(key, 33), devices)
    ranks = jax.vmap(lambda subkey: jax.random.permutation(subkey, others))(rank_keys).astype(jnp.int32)
    spare = jax.random.randint(jax.random.fold_in(key, 34), (devices,), 1, sky_count, dtype=jnp.int32)
    hot_offset = jnp.where(sky_of == hot, spare, (hot - sky_of) % sky_count)
    offsets = jnp.arange(others, dtype=jnp.int32)[None, :] + 1
    ranks = jnp.where(offsets == hot_offset[:, None], -1, ranks)
    order = (jnp.argsort(ranks, axis=1, stable=True) + 1).astype(jnp.int32)
    split_at = jax.random.randint(jax.random.fold_in(key, 35), (devices, couples), 0, BUCKET + 1, dtype=jnp.int32)
    paired = jnp.stack([split_at, BUCKET - split_at], axis=2).reshape(devices, 2 * couples)
    counts = jnp.concatenate([jnp.full((devices, 1), BUCKET, jnp.int32), paired], axis=1)
    ends = jnp.cumsum(counts, axis=1)
    position = jnp.arange(ANCHORS * PARTNERS, dtype=jnp.int32)
    which = jnp.sum((position[None, :, None] >= ends[:, None, :]).astype(jnp.int32), axis=2)
    offset = jnp.take_along_axis(order, which, axis=1)
    owner_flat = (sky_of[:, None] + offset) % sky_count
    arranged = owner_flat.reshape(devices, PARTNERS, ANCHORS).transpose(0, 2, 1)
    shuffle_keys = jax.random.split(jax.random.fold_in(key, 36), devices)
    shuffle = jax.vmap(lambda subkey: jax.random.permutation(subkey, ANCHORS))(shuffle_keys).astype(jnp.int32)
    owner = jnp.take_along_axis(arranged, shuffle[:, :, None], axis=1)
    inverse_codes = jax.vmap(lambda code: jnp.zeros((ANCHORS,), jnp.int32).at[code].set(jnp.arange(ANCHORS, dtype=jnp.int32)))(codes)
    partner_device = owner * N_LOOP + loop_of[:, None, None]
    own_code = jnp.broadcast_to(codes[:, :, None], owner.shape)
    row = inverse_codes[partner_device, own_code]
    return (owner.reshape(ROWS, PARTNERS).astype(jnp.int32), row.reshape(ROWS, PARTNERS).astype(jnp.int32))


def draw_side(key, salt):
    devices = ROWS // ANCHORS
    codes = draw_codes(key)
    loop_of = jnp.arange(devices, dtype=jnp.int32) % N_LOOP
    code_global = (loop_of[:, None] * ANCHORS + codes).reshape(ROWS)
    latent = jax.random.truncated_normal(jax.random.fold_in(key, 41), -3.0, 3.0, (N_LOOP * ANCHORS, D), jnp.float32)
    own_part = jax.random.truncated_normal(jax.random.fold_in(key, salt), -3.0, 3.0, (ROWS, D), jnp.float32)
    value = jnp.take(latent, code_global, axis=0) + 0.6 * own_part
    return jnp.clip(value / jnp.sqrt(jnp.float32(D)), -1.0, 1.0)


def draw_queries(key, part):
    return draw_side(key, 21).astype(jnp.bfloat16)


def draw_keys(key, part):
    return draw_side(key, 22).astype(jnp.bfloat16)


def draw_partner_owner(key, part):
    return draw_routes(key)[0]


def draw_partner_row(key, part):
    return draw_routes(key)[1]


def draw_partner_count(key, part):
    counts = jax.random.randint(jax.random.fold_in(key, 5), (ROWS,), 1, PARTNERS + 1, dtype=jnp.int32)
    return counts.at[0].set(PARTNERS).at[1].set(1)


def setup_inputs(seed: int = 0) -> dict:
    splits = jax.random.split(jax.random.key(seed), 6)
    return {
        "queries": draw_queries(jax.random.fold_in(splits[5], 71), 0),
        "keys": draw_keys(jax.random.fold_in(splits[5], 71), 0),
        "partner_owner": draw_partner_owner(jax.random.fold_in(splits[5], 71), 0),
        "partner_row": draw_partner_row(jax.random.fold_in(splits[5], 71), 0),
        "partner_count": draw_partner_count(jax.random.fold_in(splits[5], 71), 0),
    }


SCALE = 10.0
EPS = 1e-06

def unit_rows(rows):
    wide = rows.astype(jnp.float32)
    norms = jnp.sqrt(lax.optimization_barrier(jnp.sum(wide * wide, axis=-1, keepdims=True)) + EPS)
    return (wide / norms, norms)

def back_unit(unit, norms, grad):
    return (grad - unit * lax.optimization_barrier(jnp.sum(unit * grad, axis=-1, keepdims=True))) / norms

def reference(queries, keys, partner_owner, partner_row, partner_count):
    unit_q, norm_q = unit_rows(queries)
    unit_k, norm_k = unit_rows(keys)
    query_rows = unit_q.astype(jnp.bfloat16)
    key_rows = unit_k.astype(jnp.bfloat16)
    rows_all = jnp.arange(ROWS, dtype=jnp.int32)
    loop_place = rows_all // ANCHORS % N_LOOP
    partner_index = ((partner_owner * N_LOOP + loop_place[:, None]) * ANCHORS + partner_row).astype(jnp.int32)
    valid = jnp.arange(PARTNERS, dtype=jnp.int32)[None, :] < partner_count[:, None]
    inverse = 1.0 / (1.0 + partner_count.astype(jnp.float32))
    group_count = ROWS // GROUP

    def one_group(carry, index):
        begin = (index * GROUP).astype(jnp.int32)
        q_block = lax.dynamic_slice_in_dim(query_rows, begin, GROUP)
        k_block = lax.dynamic_slice_in_dim(key_rows, begin, GROUP)
        p_index = lax.dynamic_slice_in_dim(partner_index, begin, GROUP)
        v_block = lax.dynamic_slice_in_dim(valid, begin, GROUP)
        i_block = lax.dynamic_slice_in_dim(inverse, begin, GROUP)
        scores = SCALE * jnp.dot(q_block, k_block.T, preferred_element_type=jnp.float32)
        p_keys = jnp.take(key_rows, p_index.reshape(-1), axis=0).reshape(GROUP, PARTNERS, D)
        p_logits = SCALE * jnp.einsum('apd,ad->ap', p_keys.astype(jnp.float32), q_block.astype(jnp.float32))
        total = lax.optimization_barrier(jnp.sum(jnp.exp(scores), axis=1)) + lax.optimization_barrier(jnp.sum(jnp.where(v_block, jnp.exp(p_logits), 0.0), axis=1))
        log_total = jnp.log(total)
        loss = log_total - i_block * (jnp.diagonal(scores) + lax.optimization_barrier(jnp.sum(jnp.where(v_block, p_logits, 0.0), axis=1)))
        same = jnp.arange(GROUP, dtype=jnp.int32)[:, None] == jnp.arange(GROUP, dtype=jnp.int32)[None, :]
        weights = (jnp.exp(scores - log_total[:, None]) - jnp.where(same, i_block[:, None], 0.0)).astype(jnp.bfloat16)
        p_weights = jnp.where(v_block, jnp.exp(p_logits - log_total[:, None]) - i_block[:, None], 0.0).astype(jnp.bfloat16)
        grad_unit_q = SCALE * (jnp.dot(weights, k_block, preferred_element_type=jnp.float32) + jnp.einsum('ap,apd->ad', p_weights.astype(jnp.float32), p_keys.astype(jnp.float32)))
        loop_keys = jnp.dot(weights.T, q_block, preferred_element_type=jnp.float32)
        contrib = p_weights.astype(jnp.float32)[:, :, None] * q_block.astype(jnp.float32)[:, None, :]
        carry = carry.at[p_index.reshape(-1)].add(contrib.reshape(-1, D))
        return (carry, (loss, grad_unit_q, loop_keys))
    start = jnp.zeros((ROWS, D), jnp.float32)
    partner_grad, stacked = lax.scan(one_group, start, jnp.arange(group_count, dtype=jnp.int32))
    loss = stacked[0].reshape(ROWS)
    grad_unit_q = stacked[1].reshape(ROWS, D)
    loop_keys = stacked[2].reshape(ROWS, D)
    grad_queries = back_unit(unit_q, norm_q, grad_unit_q)
    grad_keys = back_unit(unit_k, norm_k, SCALE * (loop_keys + partner_grad))
    return (loss, grad_queries, grad_keys)
```

```python
import functools

import jax
import jax.numpy as jnp
from jax import lax
from jax.experimental import pallas as pl
from jax.experimental.pallas import tpu as pltpu
from jax.sharding import PartitionSpec as P

SCALE = 10.0
EPS = 1e-06
A = 768
D = 256
B = 192
HALF = A // 2
MESH = pl.DeviceIdType.MESH
F32 = jnp.float32
BF16 = jnp.bfloat16
I32 = jnp.int32
VMEM = pl.BlockSpec(memory_space=pltpu.VMEM)
ANY = pl.BlockSpec(memory_space=pl.ANY)


def params(**more):
    return pltpu.CompilerParams(vmem_limit_bytes=60000 * 1024, **more)


def nt(a, b):
    return lax.dot_general(a, b, (((1,), (1,)), ((), ())), preferred_element_type=F32)


def nn(a, b):
    return jnp.dot(a, b, preferred_element_type=F32)


def place():
    sky, loop = lax.axis_index("sky"), lax.axis_index("loop")
    return sky // 8, (sky // 2) % 4, sky % 2, loop // 2, loop % 2


def device(y, z, c, x):
    return ((y * 4 + z % 4) * 2 + c, x * 2 + z // 4)


def prep_kernel(q_ref, k_ref, rel_ref, row_ref, qr_ref, kr_ref, want_ref, anchor_ref, mates_ref):
    for src, dst in ((q_ref, qr_ref), (k_ref, kr_ref)):
        wide = src[...].astype(F32)
        norm = jnp.sqrt(jnp.sum(wide * wide, axis=1, keepdims=True) + EPS)
        dst[...] = (wide / norm).astype(BF16)
    sky = lax.broadcasted_iota(I32, (32, A), 0)
    hits = [rel_ref[p : p + 1, :] == sky for p in range(4)]
    hit = sum(jnp.where(h, 1.0, 0.0) for h in hits).astype(BF16)
    below = lax.broadcasted_iota(I32, (A, A), 0) < lax.broadcasted_iota(I32, (A, A), 1)
    rank = nn(hit, jnp.where(below, 1.0, 0.0).astype(BF16))
    anchor = lax.broadcasted_iota(I32, (1, A), 1) + 1
    lists = jnp.zeros((128, B), F32)
    slot = lax.broadcasted_iota(I32, (B, A), 0).astype(F32)
    for p in range(4):
        mine = jnp.sum(jnp.where(hits[p], rank, 0.0), axis=0, keepdims=True)
        chosen = jnp.where(slot == mine, 1.0, 0.0).astype(BF16)
        row = row_ref[p : p + 1, :] + 1
        parts = [anchor % 256, anchor // 256, row % 256, row // 256]
        values = jnp.concatenate(
            [jnp.where(hits[p], part.astype(F32), 0.0) for part in parts], axis=0
        ).astype(BF16)
        lists = lists + nt(values, chosen)
    anchors = (lists[0:32] + 256.0 * lists[32:64] - 1.0).astype(I32)
    wanted = (lists[64:96] + 256.0 * lists[96:128] - 1.0).astype(I32)
    anchor_ref[...] = anchors
    for dy in range(4):
        want_ref[dy] = wanted[dy * 8 : dy * 8 + 8]
        for m in range(8):
            mates_ref[m, dy : dy + 1, :] = anchors[dy * 8 + m : dy * 8 + m + 1]


def prep(queries, keys, rel, row):
    shape = jax.ShapeDtypeStruct
    return pl.pallas_call(
        prep_kernel,
        name="prep",
        out_shape=(
            shape((A, D), BF16),
            shape((A, D), BF16),
            shape((4, 8, B), I32),
            shape((32, B), I32),
            shape((8, 4, B), I32),
        ),
        in_specs=[VMEM] * 4,
        out_specs=(VMEM,) * 5,
        compiler_params=params(),
    )(queries, keys, rel, row)


def gather_kernel(k_ref, q_ref, want_ref, mates_ref, kz, qz, kc, qc, kx, qx, want_in, mates_in, send, recv, local):
    y, zl, c, x, zh = place()
    z = zh * 4 + zl
    left, right = device(y, (z + 7) % 8, c, x), device(y, (z + 1) % 8, c, x)
    xl, xr = device(y, z, c, (x + 3) % 4), device(y, z, c, (x + 1) % 4)
    sibling = device(y, z, 1 - c, x)
    across = [device((y + d) % 4, z, c, x) for d in range(4)]
    mates = [(d, f) for d in range(4) for f in range(2) if (d, f) != (0, 0)]

    def mate(d, f):
        return device(y, zh * 4 + (zl + d) % 4, (c + f) % 2, x)

    barrier = pltpu.get_barrier_semaphore()
    greeted = [left, right, xl, xr] + across[1:] + [mate(d, f) for d, f in mates]
    for other in greeted:
        pl.semaphore_signal(barrier, inc=1, device_id=other, device_id_type=MESH)
    pl.semaphore_wait(barrier, len(greeted))

    count = [0]

    def remote(src, dst, to):
        i = count[0]
        count[0] += 1
        return pltpu.make_async_remote_copy(
            src_ref=src, dst_ref=dst, send_sem=send.at[i], recv_sem=recv.at[i], device_id=to, device_id_type=MESH
        )

    started = []
    locals_ = []

    def begin(copy):
        copy.start()
        started.append(copy)
        return copy

    def begin_local(src, dst):
        copy = pltpu.make_async_copy(src, dst, local.at[len(locals_)])
        copy.start()
        locals_.append(copy)

    begin_local(want_ref.at[0], want_in.at[0])
    begin_local(mates_ref.at[zl * 2], mates_in.at[zl * 2])
    for d in range(1, 4):
        begin(remote(want_ref.at[d], want_in.at[d], across[d]))
    for d, f in mates:
        begin(remote(mates_ref.at[((zl + d) % 4) * 2 + f], mates_in.at[zl * 2 + f], mate(d, f)))

    halves = [pl.ds(0, HALF), pl.ds(HALF, HALF)]
    tensors = [(k_ref, kz, kc, kx), (q_ref, qz, qc, qx)]

    def in_run(r):
        return zl + r <= 3 if r < 4 else zl + r >= 8

    guarded = []
    for own, zbuf, cbuf, xbuf in tensors:
        begin_local(own, zbuf.at[0])
        begin_local(own, xbuf.at[0])
        flows = {}
        for step in range(4):
            for h in range(2):
                for way in range(2):
                    if step == 3 and h != way:
                        continue
                    at = step if way == 0 else (8 - step) % 8
                    to_at = at + 1 if way == 0 else (at + 7) % 8
                    src = (own if step == 0 else zbuf.at[at]).at[halves[h]]
                    dst = (xbuf.at[4] if step == 3 else zbuf.at[to_at]).at[halves[h]]
                    flows[step, h, way] = remote(src, dst, left if way == 0 else right)
        sib = {r: remote(own if r == 0 else zbuf.at[r], cbuf.at[r], sibling) for r in (0, 1, 2, 3, 5, 6, 7)}
        xs = {}
        for t in range(2):
            base = own if t == 0 else xbuf.at[4]
            xs[t, 0] = remote(base, xbuf.at[t * 4 + 3], xr)
            xs[t, 1] = remote(base, xbuf.at[t * 4 + 1], xl)
            xs[t, 2] = remote(xbuf.at[t * 4 + 3].at[halves[0]], xbuf.at[t * 4 + 2].at[halves[0]], xr)
            xs[t, 3] = remote(xbuf.at[t * 4 + 1].at[halves[1]], xbuf.at[t * 4 + 2].at[halves[1]], xl)
        for h in range(2):
            for way in range(2):
                begin(flows[0, h, way])
        begin(sib[0])
        begin(xs[0, 0])
        begin(xs[0, 1])
        for step in range(3):
            for h in range(2):
                for way in range(2):
                    flows[step, h, way].wait_recv()
                    if (step + 1, h, way) in flows:
                        begin(flows[step + 1, h, way])
            for r in (step + 1, 7 - step):
                guarded.append((r, sib[r]))

                @pl.when(in_run(r))
                def _(r=r):
                    sib[r].start()

            if step == 1:
                xs[0, 0].wait_recv()
                begin(xs[0, 2])
                xs[0, 1].wait_recv()
                begin(xs[0, 3])
        flows[3, 0, 0].wait_recv()
        flows[3, 1, 1].wait_recv()
        begin(xs[1, 0])
        begin(xs[1, 1])
        xs[1, 0].wait_recv()
        begin(xs[1, 2])
        xs[1, 1].wait_recv()
        begin(xs[1, 3])
        for key in ((0, 2), (0, 3), (1, 2), (1, 3)):
            xs[key].wait_recv()
        sib[0].wait_recv()
    for copy in started[:10]:
        copy.wait_recv()
    for copy in started:
        copy.wait_send()
    for r, copy in guarded:

        @pl.when(in_run(r))
        def _(copy=copy):
            copy.wait()

    for copy in locals_:
        copy.wait()


def gather(krows, qrows, want, mates):
    shape = jax.ShapeDtypeStruct
    block = shape((8, A, D), BF16)
    return pl.pallas_call(
        gather_kernel,
        name="gather",
        out_shape=(block,) * 6 + (shape((4, 8, B), I32), shape((8, 4, B), I32)),
        in_specs=[ANY] * 4,
        out_specs=(ANY,) * 8,
        scratch_shapes=[
            pltpu.SemaphoreType.DMA((70,)),
            pltpu.SemaphoreType.DMA((70,)),
            pltpu.SemaphoreType.DMA((8,)),
        ],
        compiler_params=params(collective_id=0, has_side_effects=True),
    )(krows, qrows, want, mates)


def select_kernel(lists_ref, same, other, out_ref, cols):
    zl = (lax.axis_index("sky") // 2) % 4
    turned = jnp.transpose(lists_ref[...].astype(F32))
    for s in range(32):
        cols[s] = jnp.broadcast_to(turned[:, s : s + 1], (B, 128))
    iota = lax.broadcasted_iota(I32, (B, A), 1).astype(F32)

    def one(s, unused):
        m = s % 8
        r = (m // 2 - zl + 8) % 8
        chosen = jnp.where(jnp.concatenate([cols[s]] * 6, axis=1) == iota, 1.0, 0.0).astype(BF16)

        @pl.when(m % 2 == 0)
        def _():
            out_ref[s] = nn(chosen, same[r]).astype(BF16)

        @pl.when(m % 2 == 1)
        def _():
            out_ref[s] = nn(chosen, other[r]).astype(BF16)

        return unused

    lax.fori_loop(0, 32, one, 0)


def select(lists, same, other):
    return pl.pallas_call(
        select_kernel,
        name="select",
        out_shape=jax.ShapeDtypeStruct((32, B, D), BF16),
        in_specs=[VMEM] * 3,
        out_specs=VMEM,
        scratch_shapes=[pltpu.VMEM((32, B, 128), F32)],
        compiler_params=params(),
    )(lists, same, other)


def cross_kernel(sk, sq, ans, qs, send, recv, local):
    y, zl, c, x, zh = place()
    z = zh * 4 + zl
    across = [device((y + d) % 4, z, c, x) for d in range(4)]
    barrier = pltpu.get_barrier_semaphore()
    for d in range(1, 4):
        pl.semaphore_signal(barrier, inc=1, device_id=across[d], device_id_type=MESH)
    pl.semaphore_wait(barrier, 3)
    copies = []
    for n, (src, dst) in enumerate(((sk, ans), (sq, qs))):
        for d in range(1, 4):
            to = across[(4 - d) % 4] if n == 0 else across[d]
            i = n * 3 + d - 1
            copy = pltpu.make_async_remote_copy(
                src_ref=src.at[d], dst_ref=dst.at[d], send_sem=send.at[i], recv_sem=recv.at[i], device_id=to, device_id_type=MESH
            )
            copy.start()
            copies.append(copy)
    own = [pltpu.make_async_copy(a.at[0], b.at[0], local.at[n]) for n, (a, b) in enumerate(((sk, ans), (sq, qs)))]
    for copy in own:
        copy.start()
    for copy in copies + own:
        copy.wait()


def cross(sk, sq):
    shape = jax.ShapeDtypeStruct((4, 8, B, D), BF16)
    return pl.pallas_call(
        cross_kernel,
        name="cross",
        out_shape=(shape, shape),
        in_specs=[ANY] * 2,
        out_specs=(ANY,) * 2,
        scratch_shapes=[pltpu.SemaphoreType.DMA((6,)), pltpu.SemaphoreType.DMA((6,)), pltpu.SemaphoreType.DMA((2,))],
        compiler_params=params(collective_id=1, has_side_effects=True),
    )(sk, sq)


ROWS = 256


def query_kernel(q_ref, qr_ref, kx, ans, anchor_ref, want_ref, count_ref, loss_ref, log_ref, grad_ref, coef_ref, hr_ref, acc, sums, own_s, tacc, tsum, tval):
    def dense(b, rows, diagonal):
        q = qr_ref[rows, :]
        s = nt(q, kx[b])
        e = jnp.exp(SCALE * s)
        if diagonal is not None:
            i = lax.broadcasted_iota(I32, (ROWS, A), 0) + diagonal
            same = i == lax.broadcasted_iota(I32, (ROWS, A), 1)
            own_s[rows, :] = SCALE * jnp.sum(jnp.where(same, s, 0.0), axis=1, keepdims=True)
            sums[rows, :] = jnp.sum(e, axis=1, keepdims=True)
            acc[rows, :] = nn(jnp.where(same, 0.0, e).astype(BF16), kx[b])
        else:
            sums[rows, :] += jnp.sum(e, axis=1, keepdims=True)
            acc[rows, :] += nn(e.astype(BF16), kx[b])

    for part in range(A // ROWS):
        dense(0, pl.ds(part * ROWS, ROWS), part * ROWS)

    def turn(n, unused):
        b, part = 1 + n // 3, n % 3
        dense(b, pl.ds(pl.multiple_of(part * ROWS, ROWS), ROWS), None)
        return unused

    lax.fori_loop(0, 21, turn, 0)

    iota = lax.broadcasted_iota(I32, (A, B), 0)
    tacc[...] = jnp.zeros_like(tacc)
    tsum[...] = jnp.zeros_like(tsum)

    def logits(s, unused):
        scores = nt(qr_ref[...], ans[s])
        match = iota == anchor_ref[pl.ds(s, 1), :]
        t = SCALE * jnp.sum(jnp.where(match, scores, 0.0), axis=0, keepdims=True)
        tval[pl.ds(s, 1), :] = t
        tacc[...] += jnp.where(match, jnp.exp(t), 0.0)
        tsum[...] += jnp.where(match, t, 0.0)
        return unused

    lax.fori_loop(0, 32, logits, 0)
    total = sums[...] + jnp.sum(tacc[...], axis=1, keepdims=True)
    log_total = jnp.log(total)
    inverse = 1.0 / (1.0 + count_ref[...].astype(F32))
    loss = log_total - inverse * (own_s[...] + jnp.sum(tsum[...], axis=1, keepdims=True))
    lane = lax.broadcasted_iota(I32, (A, 128), 1)
    turned = jnp.transpose(jnp.where(lane == 0, loss, log_total))
    loss_ref[...] = turned[0:1, :]
    log_ref[...] = turned[1:2, :]
    coef = (jnp.exp(own_s[...] - log_total) - inverse).astype(BF16).astype(F32)
    coef_ref[...] = coef
    share = 1.0 / total
    acc[...] = acc[...] * share + coef * kx[0].astype(F32)

    def weights(s, unused):
        match = iota == anchor_ref[pl.ds(s, 1), :]
        e = jnp.exp(tval[pl.ds(s, 1), :])
        w = jnp.where(match, e * share - inverse, 0.0)
        acc[...] += nn(w.astype(BF16), ans[s])
        hr_ref[s, 0:1, :] = want_ref[pl.ds(s, 1), :].astype(F32)
        hr_ref[s, 1:2, :] = jnp.sum(w, axis=0, keepdims=True)
        return unused

    lax.fori_loop(0, 32, weights, 0)
    wide = q_ref[...].astype(F32)
    norm = jnp.sqrt(jnp.sum(wide * wide, axis=1, keepdims=True) + EPS)
    unit = wide / norm
    g = SCALE * acc[...]
    grad_ref[...] = (g - unit * jnp.sum(unit * g, axis=1, keepdims=True)) / norm


def query_side(queries, qrows, kx, ans, anchors, wanted, count):
    shape = jax.ShapeDtypeStruct
    return pl.pallas_call(
        query_kernel,
        name="query_side",
        out_shape=(
            shape((1, A), F32),
            shape((1, A), F32),
            shape((A, D), F32),
            shape((A, 1), F32),
            shape((32, 2, B), F32),
        ),
        in_specs=[VMEM] * 7,
        out_specs=(VMEM,) * 5,
        scratch_shapes=[
            pltpu.VMEM((A, D), F32),
            pltpu.VMEM((A, 1), F32),
            pltpu.VMEM((A, 1), F32),
            pltpu.VMEM((A, B), F32),
            pltpu.VMEM((A, B), F32),
            pltpu.VMEM((32, B), F32),
        ],
        compiler_params=params(),
    )(queries, qrows, kx, ans, anchors, wanted, count)


def tell_kernel(log_ref, hr_ref, log_in, hr_in, send, recv, local):
    y, zl, c, x, zh = place()
    z = zh * 4 + zl
    barrier = pltpu.get_barrier_semaphore()
    loops = [(t, j) for t in range(2) for j in range(4) if (t, j) != (0, 0)]
    skies = [(d, e, f) for d in range(4) for e in range(4) for f in range(2) if (d, e, f) != (0, 0, 0)]

    def loop_peer(t, j):
        return device(y, (z + 4 * t) % 8, c, (x + 4 - j) % 4)

    def sky_peer(d, e, f):
        return device((y + d) % 4, zh * 4 + (zl + e) % 4, (c + f) % 2, x)

    greeted = [loop_peer(t, j) for t, j in loops] + [sky_peer(*s) for s in skies]
    for other in greeted:
        pl.semaphore_signal(barrier, inc=1, device_id=other, device_id_type=MESH)
    pl.semaphore_wait(barrier, len(greeted))
    copies = []

    def remote(src, dst, to):
        i = len(copies)
        copy = pltpu.make_async_remote_copy(
            src_ref=src, dst_ref=dst, send_sem=send.at[i], recv_sem=recv.at[i], device_id=to, device_id_type=MESH
        )
        copy.start()
        copies.append(copy)

    for t, j in loops:
        remote(log_ref, log_in.at[t * 4 + j], loop_peer(t, j))
    for d, e, f in skies:
        remote(hr_ref.at[d * 8 + ((zl + e) % 4) * 2 + f], hr_in.at[d * 8 + zl * 2 + f], sky_peer(d, e, f))
    own = [
        pltpu.make_async_copy(log_ref, log_in.at[0], local.at[0]),
        pltpu.make_async_copy(hr_ref.at[zl * 2], hr_in.at[zl * 2], local.at[1]),
    ]
    for copy in own:
        copy.start()
    for copy in copies + own:
        copy.wait()


def tell(logs, hr):
    shape = jax.ShapeDtypeStruct
    return pl.pallas_call(
        tell_kernel,
        name="tell",
        out_shape=(shape((8, 1, A), F32), shape((32, 2, B), F32)),
        in_specs=[ANY] * 2,
        out_specs=(ANY,) * 2,
        scratch_shapes=[pltpu.SemaphoreType.DMA((38,)), pltpu.SemaphoreType.DMA((38,)), pltpu.SemaphoreType.DMA((2,))],
        compiler_params=params(collective_id=2, has_side_effects=True),
    )(logs, hr)


def key_kernel(k_ref, kr_ref, qx, log_in, qs, hr_in, coef_ref, grad_ref, acc):
    def dense(b, rows, diagonal):
        s = nt(kr_ref[rows, :], qx[b])
        e = jnp.exp(SCALE * s - log_in[b])
        if diagonal is not None:
            i = lax.broadcasted_iota(I32, (ROWS, A), 0) + diagonal
            e = jnp.where(i == lax.broadcasted_iota(I32, (ROWS, A), 1), 0.0, e)
            acc[rows, :] = nn(e.astype(BF16), qx[b]) + coef_ref[rows, :] * qx[b, rows, :].astype(F32)
        else:
            acc[rows, :] += nn(e.astype(BF16), qx[b])

    for part in range(A // ROWS):
        dense(0, pl.ds(part * ROWS, ROWS), part * ROWS)

    def turn(n, unused):
        b, part = 1 + n // 3, n % 3
        dense(b, pl.ds(pl.multiple_of(part * ROWS, ROWS), ROWS), None)
        return unused

    lax.fori_loop(0, 21, turn, 0)
    iota = lax.broadcasted_iota(I32, (A, B), 0).astype(F32)

    def partners(s, unused):
        w = jnp.where(iota == hr_in[s, 0:1, :], hr_in[s, 1:2, :], 0.0)
        acc[...] += nn(w.astype(BF16), qs[s])
        return unused

    lax.fori_loop(0, 32, partners, 0)
    wide = k_ref[...].astype(F32)
    norm = jnp.sqrt(jnp.sum(wide * wide, axis=1, keepdims=True) + EPS)
    unit = wide / norm
    g = SCALE * acc[...]
    grad_ref[...] = (g - unit * jnp.sum(unit * g, axis=1, keepdims=True)) / norm


def key_side(keys, krows, qx, logs, qs, hr, coef):
    return pl.pallas_call(
        key_kernel,
        name="key_side",
        out_shape=jax.ShapeDtypeStruct((A, D), F32),
        in_specs=[VMEM] * 7,
        out_specs=VMEM,
        scratch_shapes=[pltpu.VMEM((A, D), F32)],
        compiler_params=params(),
    )(keys, krows, qx, logs, qs, hr, coef)


def shards(queries, keys, partner_owner, partner_row, partner_count):
    y, zl, c, x, zh = place()
    oy, oz, oc = partner_owner // 8, (partner_owner // 2) % 4, partner_owner % 2
    rel = ((oy - y + 4) % 4) * 8 + oz * 2 + (oc + c) % 2
    live = jnp.arange(4, dtype=I32)[None, :] < partner_count[:, None]
    rel = jnp.where(live, rel, -1).T
    qrows, krows, want, anchors, mates = prep(queries, keys, rel, partner_row.T)
    kz, qz, kc, qc, kx, qx, want_in, mates_in = gather(krows, qrows, want, mates)
    sk = select(want_in.reshape(32, B), kz, kc)
    sq = select(mates_in.transpose(1, 0, 2).reshape(32, B), qz, qc)
    ans, qs = cross(sk.reshape(4, 8, B, D), sq.reshape(4, 8, B, D))
    loss, logs, grad_q, coef, hr = query_side(
        queries, qrows, kx, ans.reshape(32, B, D), anchors, want.reshape(32, B), partner_count.reshape(A, 1)
    )
    log_in, hr_in = tell(logs, hr)
    grad_k = key_side(keys, krows, qx, log_in, qs.reshape(32, B, D), hr_in, coef)
    return loss.reshape(A), grad_q, grad_k


def solution(mesh):
    rows, flat = P(("sky", "loop"), None), P(("sky", "loop"))
    return jax.shard_map(
        shards,
        mesh=mesh,
        in_specs=(rows, rows, rows, rows, flat),
        out_specs=(flat, rows, rows),
        check_vma=False,
    )
```

```python
import functools

import jax
import jax.numpy as jnp
from jax import lax
from jax.experimental import pallas as pl
from jax.experimental.pallas import tpu as pltpu
from jax.sharding import PartitionSpec as P

SCALE = 10.0
EPS = 1e-06
A = 768
D = 256
B = 192
HALF = A // 2
MESH = pl.DeviceIdType.MESH
F32 = jnp.float32
BF16 = jnp.bfloat16
I32 = jnp.int32
VMEM = pl.BlockSpec(memory_space=pltpu.VMEM)
ANY = pl.BlockSpec(memory_space=pl.ANY)


def params(**more):
    return pltpu.CompilerParams(vmem_limit_bytes=60000 * 1024, **more)


def nt(a, b):
    return lax.dot_general(a, b, (((1,), (1,)), ((), ())), preferred_element_type=F32)


def nn(a, b):
    return jnp.dot(a, b, preferred_element_type=F32)


def place():
    sky, loop = lax.axis_index("sky"), lax.axis_index("loop")
    return sky // 8, (sky // 2) % 4, sky % 2, loop // 2, loop % 2


def device(y, z, c, x):
    return ((y * 4 + z % 4) * 2 + c, x * 2 + z // 4)


def prep_kernel(q_ref, k_ref, rel_ref, row_ref, qr_ref, kr_ref, want_ref, table_ref):
    for src, dst in ((q_ref, qr_ref), (k_ref, kr_ref)):
        wide = src[...].astype(F32)
        norm = jnp.sqrt(jnp.sum(wide * wide, axis=1, keepdims=True) + EPS)
        dst[...] = (wide / norm).astype(BF16)
    sky = lax.broadcasted_iota(I32, (32, A), 0)
    hits = [rel_ref[p : p + 1, :] == sky for p in range(4)]
    hit = sum(jnp.where(h, 1.0, 0.0) for h in hits).astype(BF16)
    below = lax.broadcasted_iota(I32, (A, A), 0) < lax.broadcasted_iota(I32, (A, A), 1)
    rank = nn(hit, jnp.where(below, 1.0, 0.0).astype(BF16))
    anchor = lax.broadcasted_iota(I32, (1, A), 1) + 1
    lists = jnp.zeros((128, B), F32)
    slot = lax.broadcasted_iota(I32, (B, A), 0).astype(F32)
    for p in range(4):
        mine = jnp.sum(jnp.where(hits[p], rank, 0.0), axis=0, keepdims=True)
        chosen = jnp.where(slot == mine, 1.0, 0.0).astype(BF16)
        row = row_ref[p : p + 1, :] + 1
        parts = [anchor % 256, anchor // 256, row % 256, row // 256]
        values = jnp.concatenate(
            [jnp.where(hits[p], part.astype(F32), 0.0) for part in parts], axis=0
        ).astype(BF16)
        lists = lists + nt(values, chosen)
    anchors = lists[0:32] + 256.0 * lists[32:64] - 1.0
    wanted = lists[64:96] + 256.0 * lists[96:128] - 1.0
    for d in range(4):
        want_ref[d] = wanted[d * 8 : d * 8 + 8]
    table = jnp.concatenate([anchors[d * 8 : d * 8 + 8] for d in range(4)], axis=1)
    for m in range(8):
        table_ref[m] = table[m : m + 1]


def prep(queries, keys, rel, row):
    shape = jax.ShapeDtypeStruct
    return pl.pallas_call(
        prep_kernel,
        name="prep",
        out_shape=(shape((A, D), BF16), shape((A, D), BF16), shape((4, 8, B), F32), shape((8, 1, A), F32)),
        in_specs=[VMEM] * 4,
        out_specs=(VMEM,) * 4,
        compiler_params=params(),
    )(queries, keys, rel, row)


def fold(wide):
    out = wide[:, 0:128]
    for i in range(1, wide.shape[1] // 128):
        out = out + wide[:, i * 128 : (i + 1) * 128]
    return out


def spread(narrow):
    return jnp.concatenate([narrow] * (A // 128), axis=1)


def total_kernel(
    q_ref, k_ref, qr_ref, kr_ref, want_ref, table_ref, count_ref,
    loss_ref, grad_q_ref, grad_k_ref,
    kb, qb, kx, qx, sk, sq, ans, qs, kcol, qcol, want_in, table_in,
    acc, acck, sums, tacc, tsum, own_s, share, inverse, coef, tval, log_row, log_in, hr, hr_in,
    z_send, z_recv, x_send, x_recv, c_send, c_recv, l_send, l_recv, y_send, y_recv, t_send, t_recv, local,
):
    y, zl, c, x, zh = place()
    z = zh * 4 + zl
    left, right = device(y, (z + 7) % 8, c, x), device(y, (z + 1) % 8, c, x)
    xl, xr = device(y, z, c, (x + 3) % 4), device(y, z, c, (x + 1) % 4)
    sibling = device(y, z, 1 - c, x)
    across = [device((y + d) % 4, z, c, x) for d in range(4)]
    mates = [(e, f) for e in range(4) for f in range(2) if (e, f) != (0, 0)]
    loops = [(t, j) for t in range(2) for j in range(4) if (t, j) != (0, 0)]
    skies = [(d, e, f) for d in range(4) for e in range(4) for f in range(2) if (d, e, f) != (0, 0, 0)]

    def loop_peer(t, j):
        return device(y, (z + 4 * t) % 8, c, (x + 4 - j) % 4)

    def sky_peer(d, e, f):
        return device((y + d) % 4, zh * 4 + (zl + e) % 4, (c + f) % 2, x)

    barrier = pltpu.get_barrier_semaphore()
    greeted = [left, right] + [loop_peer(*p) for p in loops] + [sky_peer(*p) for p in skies]
    for other in greeted:
        pl.semaphore_signal(barrier, inc=1, device_id=other, device_id_type=MESH)
    pl.semaphore_wait(barrier, len(greeted))

    def remote(src, dst, sends, recvs, i, to):
        return pltpu.make_async_remote_copy(
            src_ref=src, dst_ref=dst, send_sem=sends.at[i], recv_sem=recvs.at[i], device_id=to, device_id_type=MESH
        )

    owns, zs, xs = (kr_ref, qr_ref), (kb, qb), (kx, qx)
    halves = [pl.ds(0, HALF), pl.ds(HALF, HALF)]

    def z_copy(n, step, h, way):
        at = step if way == 0 else (8 - step) % 8
        to_at = at + 1 if way == 0 else (at + 7) % 8
        src = (owns[n] if step == 0 else zs[n].at[0, at]).at[halves[h]]
        dst = (xs[n].at[4] if step == 3 else zs[n].at[0, to_at]).at[halves[h]]
        return remote(src, dst, z_send, z_recv, ((n * 4 + step) * 2 + h) * 2 + way, left if way == 0 else right)

    def x_copy(n, t, kind):
        base = owns[n] if t == 0 else xs[n].at[4]
        one, two, three = (xs[n].at[t * 4 + j] for j in (1, 2, 3))
        src, dst, to = (
            (base, three, xr),
            (base, one, xl),
            (three.at[halves[0]], two.at[halves[0]], xr),
            (one.at[halves[1]], two.at[halves[1]], xl),
        )[kind]
        return remote(src, dst, x_send, x_recv, (n * 2 + t) * 4 + kind, to)

    def c_copy(n, r):
        src = owns[n] if r == 0 else zs[n].at[0, r]
        return remote(src, zs[n].at[1, r], c_send, c_recv, n * 8 + r, sibling)

    def y_copy(n, m, d):
        src, dst = ((sk, ans), (sq, qs))[n]
        rows = pl.ds(d * B, B)
        to = across[4 - d] if n == 0 else across[d]
        return remote(src.at[m, rows], dst.at[m, rows], y_send, y_recv, (n * 8 + m) * 4 + d, to)

    def list_copies():
        out = [remote(want_ref.at[d], want_in.at[d], l_send, l_recv, d, across[d]) for d in range(1, 4)]
        for e, f in mates:
            src, dst = table_ref.at[((zl + e) % 4) * 2 + f], table_in.at[zl * 2 + f]
            out.append(remote(src, dst, l_send, l_recv, 4 + e * 2 + f, sky_peer(0, e, f)))
        return out

    def log_copy(t, j):
        return remote(log_row, log_in.at[t * 4 + j], t_send, t_recv, t * 4 + j, loop_peer(t, j))

    def hr_copy(d, e, f):
        src = hr.at[(((zl + e) % 4) * 2 + f) * 4 + d]
        dst = hr_in.at[(zl * 2 + f) * 4 + d]
        return remote(src, dst, t_send, t_recv, 8 + (d * 4 + e) * 2 + f, sky_peer(d, e, f))

    def in_run(r):
        return zl + r <= 3 if r < 4 else zl + r >= 8

    def z_pass(n, step, h):
        for way in range(2):
            if step == 3 and h != way:
                continue
            z_copy(n, step, h, way).wait_recv()
            if step < 2 or (step == 2 and h == way):
                z_copy(n, step + 1, h, way).start()

    def sib(n, step, fn):
        for r in (step + 1, 7 - step):

            @pl.when(in_run(r))
            def _(r=r):
                fn(c_copy(n, r))

    def hop(step, fn):
        def one(i, unused):
            r = jnp.where(i < 2, step + 1, 7 - step)
            zz = jnp.where(i < 2, zl + step + 1, zl - step - 1)

            @pl.when((zz >= 0) & (zz <= 3))
            def _():
                fn(r, zz * 2 + i % 2, i % 2)

            return unused

        lax.fori_loop(0, 4, one, 0)

    lane_f = lax.broadcasted_iota(I32, (A, A), 1).astype(F32)
    row_f = lax.broadcasted_iota(I32, (A, A), 0).astype(F32)

    def dense_query(block, own):
        s = nt(qr_ref[...], block[...])
        e = jnp.exp(SCALE * s)
        if own:
            same = lane_f == row_f
            own_s[...] = SCALE * jnp.sum(fold(jnp.where(same, s, 0.0)), axis=1, keepdims=True)
            sums[...] = fold(e)
            acc[...] = nn(jnp.where(same, 0.0, e).astype(BF16), block[...])
        else:
            sums[...] += fold(e)
            acc[...] += nn(e.astype(BF16), block[...])

    def dense_key(block, logs, own):
        s = nt(kr_ref[...], block[...])
        e = jnp.exp(SCALE * s - logs)
        if own:
            e = jnp.where(lane_f == row_f, 0.0, e)
            acck[...] = nn(e.astype(BF16), block[...]) + coef[...] * block[...].astype(F32)
        else:
            acck[...] += nn(e.astype(BF16), block[...])

    def pick(n, m, block):
        col = (kcol, qcol)[n]
        chosen = jnp.where(spread(col[m]) == lane_f, 1.0, 0.0).astype(BF16)
        rows = nn(chosen, block[...]).astype(BF16)
        ((sk, sq)[n])[m] = rows
        ((ans, qs)[n])[m, 0:B, :] = rows[0:B]

    def pick_own(n):
        pick(n, zl * 2, owns[n])
        c_copy(n, 0).wait_recv()
        pick(n, zl * 2 + 1, zs[n].at[1, 0])

    def send_y(n, m):
        for d in range(1, 4):
            y_copy(n, m, d).start()

    def wait_y(n, m):
        for d in range(1, 4):
            y_copy(n, m, d).wait_recv()

    def pick_hop(n, step):
        sib(n, step, lambda copy: copy.wait_recv())
        hop(step, lambda r, m, g: pick(n, m, zs[n].at[g, r]))
        hop(step, lambda r, m, g: send_y(n, m))

    def logits(m):
        wait_y(0, m)
        scores = nt(qr_ref[...], ans[m])
        match = row_f == table_ref[m]
        masked = jnp.where(match, scores, 0.0)
        t = SCALE * jnp.sum(masked, axis=0, keepdims=True)
        tval[m] = t
        tsum[...] += fold(masked)
        tacc[...] += fold(jnp.where(match, jnp.exp(t), 0.0))

    def weights(m):
        match = row_f == table_ref[m]
        w = jnp.where(match, jnp.exp(tval[m]) * spread(share[...]) - spread(inverse[...]), 0.0)
        acc[...] += nn(w.astype(BF16), ans[m])
        h = jnp.sum(w, axis=0, keepdims=True)
        for d in range(4):
            hr[m * 4 + d, 1:2, :] = h[:, d * B : (d + 1) * B]

    def scatter(m):
        wait_y(1, m)
        rows = jnp.concatenate([hr_in[m * 4 + d, 0:1, :] for d in range(4)], axis=1)
        h = jnp.concatenate([hr_in[m * 4 + d, 1:2, :] for d in range(4)], axis=1)
        w = jnp.where(row_f == rows, h, 0.0)
        acck[...] += nn(w.astype(BF16), qs[m])

    def finish(src_ref, total, out_ref):
        wide = src_ref[...].astype(F32)
        norm = jnp.sqrt(jnp.sum(wide * wide, axis=1, keepdims=True) + EPS)
        unit = wide / norm
        g = SCALE * total[...]
        out_ref[...] = (g - unit * jnp.sum(unit * g, axis=1, keepdims=True)) / norm

    def own_pair(fn):
        def one(g, unused):
            fn(zl * 2 + g)
            return unused

        lax.fori_loop(0, 2, one, 0)

    def sides(t, fn):
        def one(i, unused):
            fn(t * 4 + 1 + 2 * i)
            return unused

        lax.fori_loop(0, 2, one, 0)

    for h in range(2):
        for way in range(2):
            z_copy(0, 0, h, way).start()
    lists = list_copies()
    for copy in lists:
        copy.start()
    for kind in range(2):
        x_copy(0, 0, kind).start()
    c_copy(0, 0).start()
    c_copy(1, 0).start()
    for kind in range(2):
        x_copy(1, 0, kind).start()
    own_lists = [
        pltpu.make_async_copy(want_ref.at[0], want_in.at[0], local.at[0]),
        pltpu.make_async_copy(table_ref.at[zl * 2], table_in.at[zl * 2], local.at[1]),
    ]
    for copy in own_lists:
        copy.start()
    for d in range(4):
        for m in range(8):
            hr[m * 4 + d, 0:1, :] = want_ref[d, m : m + 1, :]
    tacc[...] = jnp.zeros_like(tacc)
    tsum[...] = jnp.zeros_like(tsum)
    inverse[...] = jnp.broadcast_to(1.0 / (1.0 + count_ref[...].astype(F32)), (A, 128))
    dense_query(kr_ref, True)
    for copy in lists:
        copy.wait_recv()
    for copy in own_lists:
        copy.wait()
    for listed, cols in (
        (jnp.concatenate([want_in[d] for d in range(4)], axis=1), kcol),
        (jnp.concatenate([table_in[m] for m in range(8)], axis=0), qcol),
    ):
        turned = jnp.transpose(listed)
        for m in range(8):
            cols[m] = jnp.broadcast_to(turned[:, m : m + 1], (A, 128))
    pick_own(0)
    for g in range(2):
        send_y(0, zl * 2 + g)
    for h in range(2):
        z_pass(0, 0, h)
    sib(0, 0, lambda copy: copy.start())
    for kind in range(2):
        x_copy(0, 0, kind).wait_recv()
        x_copy(0, 0, kind + 2).start()
    sides(0, lambda b: dense_query(kx.at[b], False))
    pick_hop(0, 0)
    for h in range(2):
        z_pass(0, 1, h)
    sib(0, 1, lambda copy: copy.start())
    for kind in (2, 3):
        x_copy(0, 0, kind).wait_recv()
    dense_query(kx.at[2], False)
    for kind in range(2):
        x_copy(1, 0, kind).wait_recv()
        x_copy(1, 0, kind + 2).start()
    pick_hop(0, 1)
    for h in range(2):
        for way in range(2):
            z_copy(1, 0, h, way).start()
    pick_own(1)
    own_pair(logits)
    for h in range(2):
        z_pass(0, 2, h)
    sib(0, 2, lambda copy: copy.start())
    hop(0, lambda r, m, g: logits(m))
    pick_hop(0, 2)
    for g in range(2):
        send_y(1, zl * 2 + g)
    for h in range(2):
        z_pass(0, 3, h)
    for kind in range(2):
        x_copy(0, 1, kind).start()
    dense_query(kx.at[4], False)
    hop(1, lambda r, m, g: logits(m))
    for h in range(2):
        z_pass(1, 0, h)
    sib(1, 0, lambda copy: copy.start())
    hop(2, lambda r, m, g: logits(m))
    for kind in range(2):
        x_copy(0, 1, kind).wait_recv()
        x_copy(0, 1, kind + 2).start()
    pick_hop(1, 0)
    sides(1, lambda b: dense_query(kx.at[b], False))
    for h in range(2):
        z_pass(1, 1, h)
    sib(1, 1, lambda copy: copy.start())
    for kind in (2, 3):
        x_copy(0, 1, kind).wait_recv()
    dense_query(kx.at[6], False)

    total = jnp.sum(sums[...] + tacc[...], axis=1, keepdims=True)
    log_total = jnp.log(total)
    inv = inverse[:, 0:1]
    loss = log_total - inv * (own_s[...] + SCALE * jnp.sum(tsum[...], axis=1, keepdims=True))
    lane = lax.broadcasted_iota(I32, (A, 128), 1)
    turned = jnp.transpose(jnp.where(lane == 0, loss, log_total))
    loss_ref[...] = turned[0:1, :]
    log_row[...] = turned[1:2, :]
    mine = (jnp.exp(own_s[...] - log_total) - inv).astype(BF16).astype(F32)
    coef[...] = mine
    share[...] = jnp.broadcast_to(1.0 / total, (A, 128))
    acc[...] = acc[...] * (1.0 / total) + mine * kr_ref[...].astype(F32)
    weights(0)
    for t, j in loops:
        log_copy(t, j).start()

    def more(m, unused):
        weights(m)
        return unused

    lax.fori_loop(1, 8, more, 0)
    for h in range(2):
        z_pass(1, 2, h)
    sib(1, 2, lambda copy: copy.start())
    pick_hop(1, 1)
    for sky in skies:
        hr_copy(*sky).start()
    own_hr = [
        pltpu.make_async_copy(hr.at[(zl * 2) * 4], hr_in.at[(zl * 2) * 4], local.at[2]),
    ]
    for copy in own_hr:
        copy.start()
    dense_key(qr_ref, log_row[...], True)
    pick_hop(1, 2)
    for h in range(2):
        z_pass(1, 3, h)
    for kind in range(2):
        x_copy(1, 1, kind).start()
    for kind in (2, 3):
        x_copy(1, 0, kind).wait_recv()
    for t, j in loops:
        log_copy(t, j).wait_recv()

    def near(j, unused):
        dense_key(qx.at[j], log_in[j], False)
        return unused

    lax.fori_loop(1, 5, near, 0)
    finish(q_ref, acc, grad_q_ref)
    for copy in own_hr:
        copy.wait()
    for sky in skies:
        hr_copy(*sky).wait_recv()
    for kind in range(2):
        x_copy(1, 1, kind).wait_recv()
        x_copy(1, 1, kind + 2).start()
    own_pair(scatter)
    hop(0, lambda r, m, g: scatter(m))
    sides(1, lambda b: dense_key(qx.at[b], log_in[b], False))
    hop(1, lambda r, m, g: scatter(m))
    for kind in (2, 3):
        x_copy(1, 1, kind).wait_recv()
    dense_key(qx.at[6], log_in[6], False)
    hop(2, lambda r, m, g: scatter(m))
    finish(k_ref, acck, grad_k_ref)

    for copy in lists:
        copy.wait_send()
    for n in range(2):
        for step in range(4):
            for h in range(2):
                for way in range(2):
                    if step < 3 or h == way:
                        z_copy(n, step, h, way).wait_send()
        for t in range(2):
            for kind in range(4):
                x_copy(n, t, kind).wait_send()
        c_copy(n, 0).wait_send()
        for step in range(3):
            sib(n, step, lambda copy: copy.wait_send())
        for m in range(8):
            for d in range(1, 4):
                y_copy(n, m, d).wait_send()
    for t, j in loops:
        log_copy(t, j).wait_send()
    for sky in skies:
        hr_copy(*sky).wait_send()


def everything(queries, keys, qrows, krows, want, table, count):
    shape = jax.ShapeDtypeStruct
    vm = pltpu.VMEM
    dma = pltpu.SemaphoreType.DMA
    eight = vm((8, A, D), BF16)
    both = vm((2, 8, A, D), BF16)
    column = vm((A, 1), F32)
    narrow = vm((A, 128), F32)
    return pl.pallas_call(
        total_kernel,
        name="everything",
        out_shape=(shape((1, A), F32), shape((A, D), F32), shape((A, D), F32)),
        in_specs=[VMEM] * 7,
        out_specs=(VMEM,) * 3,
        scratch_shapes=[both, both]
        + [eight] * 6
        + [vm((8, A, 128), F32)] * 2
        + [vm((4, 8, B), F32), vm((8, 1, A), F32)]
        + [vm((A, D), F32)] * 2
        + [narrow] * 3
        + [column, narrow, narrow, column]
        + [vm((8, 1, A), F32), vm((1, A), F32), vm((8, 1, A), F32)]
        + [vm((32, 2, B), F32)] * 2
        + [dma((32,))] * 2
        + [dma((16,))] * 2
        + [dma((16,))] * 2
        + [dma((12,))] * 2
        + [dma((64,))] * 2
        + [dma((40,))] * 2
        + [dma((3,))],
        compiler_params=params(collective_id=0, has_side_effects=True),
    )(queries, keys, qrows, krows, want, table, count)


def shards(queries, keys, partner_owner, partner_row, partner_count):
    y, zl, c, x, zh = place()
    oy, oz, oc = partner_owner // 8, (partner_owner // 2) % 4, partner_owner % 2
    rel = ((oy - y + 4) % 4) * 8 + oz * 2 + (oc + c) % 2
    live = jnp.arange(4, dtype=I32)[None, :] < partner_count[:, None]
    rel = jnp.where(live, rel, -1).T
    qrows, krows, want, table = prep(queries, keys, rel, partner_row.T)
    loss, grad_q, grad_k = everything(queries, keys, qrows, krows, want, table, partner_count.reshape(A, 1))
    return loss.reshape(A), grad_q, grad_k


def solution(mesh):
    rows, flat = P(("sky", "loop"), None), P(("sky", "loop"))
    return jax.shard_map(
        shards,
        mesh=mesh,
        in_specs=(rows, rows, rows, rows, flat),
        out_specs=(flat, rows, rows),
        check_vma=False,
    )
```

```python
import functools

import jax
import jax.numpy as jnp
from jax import lax
from jax.experimental import pallas as pl
from jax.experimental.pallas import tpu as pltpu
from jax.sharding import PartitionSpec as P

SCALE = 10.0
EPS = 1e-06
A = 768
D = 256
B = 192
HALF = A // 2
MESH = pl.DeviceIdType.MESH
F32 = jnp.float32
BF16 = jnp.bfloat16
I32 = jnp.int32
VMEM = pl.BlockSpec(memory_space=pltpu.VMEM)
ANY = pl.BlockSpec(memory_space=pl.ANY)


def params(**more):
    return pltpu.CompilerParams(vmem_limit_bytes=60000 * 1024, **more)


def nt(a, b):
    return lax.dot_general(a, b, (((1,), (1,)), ((), ())), preferred_element_type=F32)


def nn(a, b):
    return jnp.dot(a, b, preferred_element_type=F32)


def place():
    sky, loop = lax.axis_index("sky"), lax.axis_index("loop")
    return sky // 8, (sky // 2) % 4, sky % 2, loop // 2, loop % 2


def device(y, z, c, x):
    return ((y * 4 + z % 4) * 2 + c, x * 2 + z // 4)


def unit_block(src, dst):
    wide = src[...].astype(F32)
    norm = jnp.sqrt(jnp.sum(wide * wide, axis=1, keepdims=True) + EPS)
    dst[...] = (wide / norm).astype(BF16)


def slot_lists(rel_ref, row_ref, want_ref, table_ref):
    sky = lax.broadcasted_iota(I32, (32, A), 0)
    hits = [rel_ref[p : p + 1, :] == sky for p in range(4)]
    hit = sum(jnp.where(h, 1.0, 0.0) for h in hits).astype(BF16)
    below = lax.broadcasted_iota(I32, (A, A), 0) < lax.broadcasted_iota(I32, (A, A), 1)
    rank = nn(hit, jnp.where(below, 1.0, 0.0).astype(BF16))
    anchor = lax.broadcasted_iota(I32, (1, A), 1) + 1
    lists = jnp.zeros((128, B), F32)
    slot = lax.broadcasted_iota(I32, (B, A), 0).astype(F32)
    for p in range(4):
        mine = jnp.sum(jnp.where(hits[p], rank, 0.0), axis=0, keepdims=True)
        chosen = jnp.where(slot == mine, 1.0, 0.0).astype(BF16)
        row = row_ref[p : p + 1, :] + 1
        parts = [anchor % 256, anchor // 256, row % 256, row // 256]
        values = jnp.concatenate(
            [jnp.where(hits[p], part.astype(F32), 0.0) for part in parts], axis=0
        ).astype(BF16)
        lists = lists + nt(values, chosen)
    anchors = lists[0:32] + 256.0 * lists[32:64] - 1.0
    wanted = lists[64:96] + 256.0 * lists[96:128] - 1.0
    for d in range(4):
        want_ref[d] = wanted[d * 8 : d * 8 + 8]
    table = jnp.concatenate([anchors[d * 8 : d * 8 + 8] for d in range(4)], axis=1)
    for m in range(8):
        table_ref[m] = table[m : m + 1]


def fold(wide):
    out = wide[:, 0:128]
    for i in range(1, wide.shape[1] // 128):
        out = out + wide[:, i * 128 : (i + 1) * 128]
    return out


def spread(narrow):
    return jnp.concatenate([narrow] * (A // 128), axis=1)


def total_kernel(
    q_ref, k_ref, rel_ref, row_ref, count_ref,
    loss_ref, grad_q_ref, grad_k_ref,
    qr_ref, kr_ref, want_ref, table_ref,
    kb, qb, kx, qx, sk, sq, ans, qs, kcol, qcol, want_in, table_in,
    acc, acck, sums, tacc, tsum, own_s, share, inverse, coef, tval, log_row, log_in, hr, hr_in,
    z_send, z_recv, x_send, x_recv, c_send, c_recv, l_send, l_recv, y_send, y_recv, t_send, t_recv, local,
):
    y, zl, c, x, zh = place()
    z = zh * 4 + zl
    left, right = device(y, (z + 7) % 8, c, x), device(y, (z + 1) % 8, c, x)
    xl, xr = device(y, z, c, (x + 3) % 4), device(y, z, c, (x + 1) % 4)
    sibling = device(y, z, 1 - c, x)
    across = [device((y + d) % 4, z, c, x) for d in range(4)]
    mates = [(e, f) for e in range(4) for f in range(2) if (e, f) != (0, 0)]
    loops = [(t, j) for t in range(2) for j in range(4) if (t, j) != (0, 0)]
    skies = [(d, e, f) for d in range(4) for e in range(4) for f in range(2) if (d, e, f) != (0, 0, 0)]

    def loop_peer(t, j):
        return device(y, (z + 4 * t) % 8, c, (x + 4 - j) % 4)

    def sky_peer(d, e, f):
        return device((y + d) % 4, zh * 4 + (zl + e) % 4, (c + f) % 2, x)

    barrier = pltpu.get_barrier_semaphore()
    greeted = [left, right, xl, xr] + across[1:] + [sky_peer(0, *p) for p in mates]
    for other in greeted:
        pl.semaphore_signal(barrier, inc=1, device_id=other, device_id_type=MESH)
    unit_block(k_ref, kr_ref)
    unit_block(q_ref, qr_ref)
    slot_lists(rel_ref, row_ref, want_ref, table_ref)
    pair = jnp.concatenate([count_ref[...].astype(F32), table_ref[zl * 2]] + [jnp.zeros((6, A), F32)], axis=0)
    turned = jnp.transpose(pair)
    inverse[...] = jnp.broadcast_to(1.0 / (1.0 + turned[:, 0:1]), (A, 128))
    qcol[zl * 2] = jnp.broadcast_to(turned[:, 1:2], (A, 128))
    for d in range(4):
        for m in range(8):
            hr[m * 4 + d, 0:1, :] = want_ref[d, m : m + 1, :]
    tacc[...] = jnp.zeros_like(tacc)
    tsum[...] = jnp.zeros_like(tsum)

    def remote(src, dst, sends, recvs, i, to):
        return pltpu.make_async_remote_copy(
            src_ref=src, dst_ref=dst, send_sem=sends.at[i], recv_sem=recvs.at[i], device_id=to, device_id_type=MESH
        )

    owns, zs, xs = (kr_ref, qr_ref), (kb, qb), (kx, qx)
    halves = [pl.ds(0, HALF), pl.ds(HALF, HALF)]

    def z_copy(n, step, h, way):
        at = step if way == 0 else (8 - step) % 8
        to_at = at + 1 if way == 0 else (at + 7) % 8
        src = (owns[n] if step == 0 else zs[n].at[0, at]).at[halves[h]]
        dst = (xs[n].at[4] if step == 3 else zs[n].at[0, to_at]).at[halves[h]]
        return remote(src, dst, z_send, z_recv, ((n * 4 + step) * 2 + h) * 2 + way, left if way == 0 else right)

    def x_copy(n, t, kind):
        base = owns[n] if t == 0 else xs[n].at[4]
        one, two, three = (xs[n].at[t * 4 + j] for j in (1, 2, 3))
        src, dst, to = (
            (base, three, xr),
            (base, one, xl),
            (three.at[halves[0]], two.at[halves[0]], xr),
            (one.at[halves[1]], two.at[halves[1]], xl),
        )[kind]
        return remote(src, dst, x_send, x_recv, (n * 2 + t) * 4 + kind, to)

    def c_copy(n, r):
        src = owns[n] if r == 0 else zs[n].at[0, r]
        return remote(src, zs[n].at[1, r], c_send, c_recv, n * 8 + r, sibling)

    def y_copy(n, m, d):
        src, dst = ((sk, ans), (sq, qs))[n]
        rows = pl.ds(d * B, B)
        to = across[4 - d] if n == 0 else across[d]
        return remote(src.at[m, rows], dst.at[m, rows], y_send, y_recv, (n * 8 + m) * 4 + d, to)

    def list_copies():
        out = [remote(want_ref.at[d], want_in.at[d], l_send, l_recv, d, across[d]) for d in range(1, 4)]
        for e, f in mates:
            src, dst = table_ref.at[((zl + e) % 4) * 2 + f], table_in.at[zl * 2 + f]
            out.append(remote(src, dst, l_send, l_recv, 4 + e * 2 + f, sky_peer(0, e, f)))
        return out

    def log_copy(t, j):
        return remote(log_row, log_in.at[t * 4 + j], t_send, t_recv, t * 4 + j, loop_peer(t, j))

    def hr_copy(d, e, f):
        src = hr.at[(((zl + e) % 4) * 2 + f) * 4 + d]
        dst = hr_in.at[(zl * 2 + f) * 4 + d]
        return remote(src, dst, t_send, t_recv, 8 + (d * 4 + e) * 2 + f, sky_peer(d, e, f))

    def in_run(r):
        return zl + r <= 3 if r < 4 else zl + r >= 8

    def reaches(step, way):
        src = (zl + step) % 4 if way == 0 else (zl + 8 - step) % 4
        far = src >= 2 if way == 0 else src < 2
        return jnp.where(far, 4, src if way == 0 else 3 - src)

    def z_each(n, step, h, fn):
        for way in range(2):

            @pl.when(reaches(step, way) > step)
            def _(way=way):
                fn(z_copy(n, step, h, way))

    def z_start(n):
        for h in range(2):
            z_each(n, 0, h, lambda copy: copy.start())

    def z_pass(n, step, h):
        for way in range(2):
            hops = reaches(step + 1, way)

            @pl.when(hops > step)
            def _(way=way):
                z_copy(n, step, h, way).wait_recv()

            if step < 3:

                @pl.when(hops > step + 1)
                def _(way=way):
                    z_copy(n, step + 1, h, way).start()

    def sib(n, step, fn):
        for r in (step + 1, 7 - step):

            @pl.when(in_run(r))
            def _(r=r):
                fn(c_copy(n, r))

    def hop(step, fn):
        def one(i, unused):
            r = jnp.where(i < 2, step + 1, 7 - step)
            zz = jnp.where(i < 2, zl + step + 1, zl - step - 1)

            @pl.when((zz >= 0) & (zz <= 3))
            def _():
                fn(r, zz * 2 + i % 2, i % 2)

            return unused

        lax.fori_loop(0, 4, one, 0)

    lane_f = lax.broadcasted_iota(I32, (A, A), 1).astype(F32)
    row_f = lax.broadcasted_iota(I32, (A, A), 0).astype(F32)

    def dense_query(block, own):
        s = nt(qr_ref[...], block[...])
        e = jnp.exp(SCALE * s)
        if own:
            same = lane_f == row_f
            own_s[...] = SCALE * jnp.sum(fold(jnp.where(same, s, 0.0)), axis=1, keepdims=True)
            sums[...] = fold(e)
            acc[...] = nn(jnp.where(same, 0.0, e).astype(BF16), block[...])
        else:
            sums[...] += fold(e)
            acc[...] += nn(e.astype(BF16), block[...])

    def dense_key(block, logs, own):
        s = nt(kr_ref[...], block[...])
        e = jnp.exp(SCALE * s - logs)
        if own:
            e = jnp.where(lane_f == row_f, 0.0, e)
            acck[...] = nn(e.astype(BF16), block[...]) + coef[...] * block[...].astype(F32)
        else:
            acck[...] += nn(e.astype(BF16), block[...])

    def pick(n, m, block):
        col = (kcol, qcol)[n]
        chosen = jnp.where(spread(col[m]) == lane_f, 1.0, 0.0).astype(BF16)
        rows = nn(chosen, block[...]).astype(BF16)
        ((sk, sq)[n])[m] = rows
        ((ans, qs)[n])[m, 0:B, :] = rows[0:B]

    def send_y(n, m):
        for d in range(1, 4):
            y_copy(n, m, d).start()

    def wait_y(n, m):
        for d in range(1, 4):
            y_copy(n, m, d).wait_recv()

    def pick_hop(n, step):
        sib(n, step, lambda copy: copy.wait_recv())
        hop(step, lambda r, m, g: pick(n, m, zs[n].at[g, r]))
        hop(step, lambda r, m, g: send_y(n, m))

    def logits(m):
        wait_y(0, m)
        scores = nt(qr_ref[...], ans[m])
        match = row_f == table_ref[m]
        masked = jnp.where(match, scores, 0.0)
        t = SCALE * jnp.sum(masked, axis=0, keepdims=True)
        tval[m] = t
        tsum[...] += fold(masked)
        tacc[...] += fold(jnp.where(match, jnp.exp(t), 0.0))

    def weights(m):
        match = row_f == table_ref[m]
        w = jnp.where(match, jnp.exp(tval[m]) * spread(share[...]) - spread(inverse[...]), 0.0)
        acc[...] += nn(w.astype(BF16), ans[m])
        h = jnp.sum(w, axis=0, keepdims=True)
        for d in range(4):
            hr[m * 4 + d, 1:2, :] = h[:, d * B : (d + 1) * B]

    def scatter(m):
        wait_y(1, m)
        rows = jnp.concatenate([hr_in[m * 4 + d, 0:1, :] for d in range(4)], axis=1)
        h = jnp.concatenate([hr_in[m * 4 + d, 1:2, :] for d in range(4)], axis=1)
        w = jnp.where(row_f == rows, h, 0.0)
        acck[...] += nn(w.astype(BF16), qs[m])

    def finish(src_ref, total, out_ref):
        wide = src_ref[...].astype(F32)
        norm = jnp.sqrt(jnp.sum(wide * wide, axis=1, keepdims=True) + EPS)
        unit = wide / norm
        g = SCALE * total[...]
        out_ref[...] = (g - unit * jnp.sum(unit * g, axis=1, keepdims=True)) / norm

    def own_pair(fn):
        def one(g, unused):
            fn(zl * 2 + g)
            return unused

        lax.fori_loop(0, 2, one, 0)

    def z_step(n, step):
        for h in range(2):
            z_pass(n, step, h)
        if step < 3:
            sib(n, step, lambda copy: copy.start())

    def x_start(n, t):
        for kind in range(2):
            x_copy(n, t, kind).start()

    def x_turn(n, t):
        for kind in range(2):
            x_copy(n, t, kind).wait_recv()
            x_copy(n, t, kind + 2).start()

    def x_end(n, t):
        for kind in (2, 3):
            x_copy(n, t, kind).wait_recv()

    def sides(t, fn):
        def one(i, unused):
            fn(t * 4 + 1 + 2 * i)
            return unused

        lax.fori_loop(0, 2, one, 0)

    pick(1, zl * 2, qr_ref)
    pl.semaphore_wait(barrier, len(greeted))
    lists = list_copies()
    for copy in lists:
        copy.start()
    send_y(1, zl * 2)
    z_start(0)
    x_start(0, 0)
    c_copy(0, 0).start()
    c_copy(1, 0).start()
    own_lists = [
        pltpu.make_async_copy(want_ref.at[0], want_in.at[0], local.at[0]),
        pltpu.make_async_copy(table_ref.at[zl * 2], table_in.at[zl * 2], local.at[1]),
    ]
    for copy in own_lists:
        copy.start()
    dense_query(kr_ref, True)
    for copy in lists:
        copy.wait_recv()
    for copy in own_lists:
        copy.wait()
    for listed, cols in (
        (jnp.concatenate([want_in[d] for d in range(4)], axis=1), kcol),
        (jnp.concatenate([table_in[m] for m in range(8)], axis=0), qcol),
    ):
        turned = jnp.transpose(listed)
        for m in range(8):
            cols[m] = jnp.broadcast_to(turned[:, m : m + 1], (A, 128))
    pick(0, zl * 2, kr_ref)
    c_copy(0, 0).wait_recv()
    pick(0, zl * 2 + 1, kb.at[1, 0])
    for g in range(2):
        send_y(0, zl * 2 + g)
    c_copy(1, 0).wait_recv()
    pick(1, zl * 2 + 1, qb.at[1, 0])
    send_y(1, zl * 2 + 1)
    z_step(0, 0)
    x_turn(0, 0)
    x_start(1, 0)
    sides(0, lambda b: dense_query(kx.at[b], False))
    pick_hop(0, 0)
    z_step(0, 1)
    z_start(1)
    x_end(0, 0)
    dense_query(kx.at[2], False)
    pick_hop(0, 1)
    x_turn(1, 0)
    own_pair(logits)
    z_step(0, 2)
    z_step(1, 0)
    pick_hop(0, 2)
    z_step(0, 3)
    x_start(0, 1)
    dense_query(kx.at[4], False)
    pick_hop(1, 0)
    z_step(1, 1)
    hop(0, lambda r, m, g: logits(m))
    x_turn(0, 1)
    sides(1, lambda b: dense_query(kx.at[b], False))
    pick_hop(1, 1)
    z_step(1, 2)
    x_end(0, 1)
    dense_query(kx.at[6], False)
    hop(1, lambda r, m, g: logits(m))
    pick_hop(1, 2)
    z_step(1, 3)
    x_start(1, 1)
    hop(2, lambda r, m, g: logits(m))

    total = jnp.sum(sums[...] + tacc[...], axis=1, keepdims=True)
    log_total = jnp.log(total)
    inv = inverse[:, 0:1]
    loss = log_total - inv * (own_s[...] + SCALE * jnp.sum(tsum[...], axis=1, keepdims=True))
    lane = lax.broadcasted_iota(I32, (A, 128), 1)
    turned = jnp.transpose(jnp.where(lane == 0, loss, log_total))
    loss_ref[...] = turned[0:1, :]
    log_row[...] = turned[1:2, :]
    mine = (jnp.exp(own_s[...] - log_total) - inv).astype(BF16).astype(F32)
    coef[...] = mine
    share[...] = jnp.broadcast_to(1.0 / total, (A, 128))
    acc[...] = acc[...] * (1.0 / total) + mine * kr_ref[...].astype(F32)
    weights(0)
    for t, j in loops:
        log_copy(t, j).start()

    def more(m, unused):
        weights(m)
        return unused

    lax.fori_loop(1, 8, more, 0)
    for sky in skies:
        hr_copy(*sky).start()
    own_hr = pltpu.make_async_copy(hr.at[(zl * 2) * 4], hr_in.at[(zl * 2) * 4], local.at[2])
    own_hr.start()
    dense_key(qr_ref, log_row[...], True)
    x_end(1, 0)
    for t, j in loops:
        log_copy(t, j).wait_recv()

    def near(j, unused):
        dense_key(qx.at[j], log_in[j], False)
        return unused

    lax.fori_loop(1, 5, near, 0)
    x_turn(1, 1)
    finish(q_ref, acc, grad_q_ref)
    own_hr.wait()
    for sky in skies:
        hr_copy(*sky).wait_recv()
    own_pair(scatter)
    hop(0, lambda r, m, g: scatter(m))
    sides(1, lambda b: dense_key(qx.at[b], log_in[b], False))
    x_end(1, 1)
    dense_key(qx.at[6], log_in[6], False)
    hop(1, lambda r, m, g: scatter(m))
    hop(2, lambda r, m, g: scatter(m))
    finish(k_ref, acck, grad_k_ref)

    for copy in lists:
        copy.wait_send()
    for n in range(2):
        for step in range(4):
            for h in range(2):
                z_each(n, step, h, lambda copy: copy.wait_send())
        for t in range(2):
            for kind in range(4):
                x_copy(n, t, kind).wait_send()
        c_copy(n, 0).wait_send()
        for step in range(3):
            sib(n, step, lambda copy: copy.wait_send())
        for m in range(8):
            for d in range(1, 4):
                y_copy(n, m, d).wait_send()
    for t, j in loops:
        log_copy(t, j).wait_send()
    for sky in skies:
        hr_copy(*sky).wait_send()


def everything(queries, keys, rel, row, count):
    shape = jax.ShapeDtypeStruct
    vm = pltpu.VMEM
    dma = pltpu.SemaphoreType.DMA
    eight = vm((8, A, D), BF16)
    both = vm((2, 8, A, D), BF16)
    column = vm((A, 1), F32)
    narrow = vm((A, 128), F32)
    return pl.pallas_call(
        total_kernel,
        name="everything",
        out_shape=(shape((1, A), F32), shape((A, D), F32), shape((A, D), F32)),
        in_specs=[VMEM] * 5,
        out_specs=(VMEM,) * 3,
        scratch_shapes=[vm((A, D), BF16)] * 2
        + [vm((4, 8, B), F32), vm((8, 1, A), F32)]
        + [both, both]
        + [eight] * 6
        + [vm((8, A, 128), F32)] * 2
        + [vm((4, 8, B), F32), vm((8, 1, A), F32)]
        + [vm((A, D), F32)] * 2
        + [narrow] * 3
        + [column, narrow, narrow, column]
        + [vm((8, 1, A), F32), vm((1, A), F32), vm((8, 1, A), F32)]
        + [vm((32, 2, B), F32)] * 2
        + [dma((32,))] * 2
        + [dma((16,))] * 2
        + [dma((16,))] * 2
        + [dma((12,))] * 2
        + [dma((64,))] * 2
        + [dma((40,))] * 2
        + [dma((3,))],
        compiler_params=params(collective_id=0, has_side_effects=True),
    )(queries, keys, rel, row, count)


def shards(queries, keys, partner_owner, partner_row, partner_count):
    y, zl, c, x, zh = place()
    oy, oz, oc = partner_owner // 8, (partner_owner // 2) % 4, partner_owner % 2
    rel = ((oy - y + 4) % 4) * 8 + oz * 2 + (oc + c) % 2
    live = jnp.arange(4, dtype=I32)[None, :] < partner_count[:, None]
    rel = jnp.where(live, rel, -1).T
    loss, grad_q, grad_k = everything(queries, keys, rel, partner_row.T, partner_count.reshape(1, A))
    return loss.reshape(A), grad_q, grad_k


def solution(mesh):
    rows, flat = P(("sky", "loop"), None), P(("sky", "loop"))
    return jax.shard_map(
        shards,
        mesh=mesh,
        in_specs=(rows, rows, rows, rows, flat),
        out_specs=(flat, rows, rows),
        check_vma=False,
    )
```

```python
import functools

import jax
import jax.numpy as jnp
from jax import lax
from jax.experimental import pallas as pl
from jax.experimental.pallas import tpu as pltpu
from jax.sharding import PartitionSpec as P

SCALE = 10.0
EPS = 1e-06
A = 768
D = 256
B = 192
HALF = A // 2
PIECES = 4
MESH = pl.DeviceIdType.MESH
F32 = jnp.float32
BF16 = jnp.bfloat16
I32 = jnp.int32
VMEM = pl.BlockSpec(memory_space=pltpu.VMEM)
ANY = pl.BlockSpec(memory_space=pl.ANY)


def params(**more):
    return pltpu.CompilerParams(vmem_limit_bytes=60000 * 1024, **more)


def nt(a, b):
    return lax.dot_general(a, b, (((1,), (1,)), ((), ())), preferred_element_type=F32)


def nn(a, b):
    return jnp.dot(a, b, preferred_element_type=F32)


def place():
    sky, loop = lax.axis_index("sky"), lax.axis_index("loop")
    return sky // 8, (sky // 2) % 4, sky % 2, loop // 2, loop % 2


def device(y, z, c, x):
    return ((y * 4 + z % 4) * 2 + c, x * 2 + z // 4)


def unit_block(src, dst):
    wide = src[...].astype(F32)
    norm = jnp.sqrt(jnp.sum(wide * wide, axis=1, keepdims=True) + EPS)
    dst[...] = (wide / norm).astype(BF16)


def slot_lists(rel, row_ref, want_ref, table_ref):
    sky = lax.broadcasted_iota(I32, (32, A), 0)
    hits = [rel[p : p + 1, :] == sky for p in range(4)]
    hit = sum(jnp.where(h, 1.0, 0.0) for h in hits).astype(BF16)
    below = lax.broadcasted_iota(I32, (A, A), 0) < lax.broadcasted_iota(I32, (A, A), 1)
    rank = nn(hit, jnp.where(below, 1.0, 0.0).astype(BF16))
    anchor = lax.broadcasted_iota(I32, (1, A), 1) + 1
    lists = jnp.zeros((128, B), F32)
    slot = lax.broadcasted_iota(I32, (B, A), 0).astype(F32)
    for p in range(4):
        mine = jnp.sum(jnp.where(hits[p], rank, 0.0), axis=0, keepdims=True)
        chosen = jnp.where(slot == mine, 1.0, 0.0).astype(BF16)
        row = row_ref[p : p + 1, :] + 1
        parts = [anchor % 256, anchor // 256, row % 256, row // 256]
        values = jnp.concatenate(
            [jnp.where(hits[p], part.astype(F32), 0.0) for part in parts], axis=0
        ).astype(BF16)
        lists = lists + nt(values, chosen)
    anchors = lists[0:32] + 256.0 * lists[32:64] - 1.0
    wanted = lists[64:96] + 256.0 * lists[96:128] - 1.0
    for d in range(4):
        want_ref[d] = wanted[d * 8 : d * 8 + 8]
    table = jnp.concatenate([anchors[d * 8 : d * 8 + 8] for d in range(4)], axis=1)
    for m in range(8):
        table_ref[m] = table[m : m + 1]


def fold(wide):
    out = wide[:, 0:128]
    for i in range(1, wide.shape[1] // 128):
        out = out + wide[:, i * 128 : (i + 1) * 128]
    return out


def spread(narrow):
    return jnp.concatenate([narrow] * (A // 128), axis=1)


def total_kernel(
    q_ref, k_ref, owner_ref, row_ref, count_ref,
    loss_ref, acc, acck,
    qr_ref, kr_ref, want_ref, table_ref,
    kb, qb, kx, qx, sk, sq, ans, qs, kcol, qcol, want_in, table_in,
    sums, tacc, tsum, own_s, share, inverse, coef, tval, log_row, log_in, hr, hr_in,
    z_send, z_recv, x_send, x_recv, c_send, c_recv, l_send, l_recv, y_send, y_recv, t_send, t_recv, local,
):
    y, zl, c, x, zh = place()
    z = zh * 4 + zl
    left, right = device(y, (z + 7) % 8, c, x), device(y, (z + 1) % 8, c, x)
    xl, xr = device(y, z, c, (x + 3) % 4), device(y, z, c, (x + 1) % 4)
    sibling = device(y, z, 1 - c, x)
    across = [device((y + d) % 4, z, c, x) for d in range(4)]
    mates = [(e, f) for e in range(4) for f in range(2) if (e, f) != (0, 0)]
    loops = [(t, j) for t in range(2) for j in range(4) if (t, j) != (0, 0)]
    skies = [(d, e, f) for d in range(4) for e in range(4) for f in range(2) if (d, e, f) != (0, 0, 0)]

    def loop_peer(t, j):
        return device(y, (z + 4 * t) % 8, c, (x + 4 - j) % 4)

    def sky_peer(d, e, f):
        return device((y + d) % 4, zh * 4 + (zl + e) % 4, (c + f) % 2, x)

    barrier = pltpu.get_barrier_semaphore()
    greeted = [left, right, xl, xr] + across[1:] + [sky_peer(0, *p) for p in mates]
    for other in greeted:
        pl.semaphore_signal(barrier, inc=1, device_id=other, device_id_type=MESH)
    unit_block(k_ref, kr_ref)
    unit_block(q_ref, qr_ref)
    owner, count = owner_ref[...], count_ref[...].reshape(1, A)
    rel = ((owner // 8 - y + 4) % 4) * 8 + owner % 8 // 2 * 2 + (owner + c) % 2
    rel = jnp.where(lax.broadcasted_iota(I32, (4, A), 0) < count, rel, -1)
    slot_lists(rel, row_ref, want_ref, table_ref)
    pair = jnp.concatenate([count.astype(F32), table_ref[zl * 2]] + [jnp.zeros((6, A), F32)], axis=0)
    turned = jnp.transpose(pair)
    inverse[...] = jnp.broadcast_to(1.0 / (1.0 + turned[:, 0:1]), (A, 128))
    qcol[zl * 2] = jnp.broadcast_to(turned[:, 1:2], (A, 128))
    for d in range(4):
        for m in range(8):
            hr[m * 4 + d, 0:1, :] = want_ref[d, m : m + 1, :]
    tacc[...] = jnp.zeros_like(tacc)
    tsum[...] = jnp.zeros_like(tsum)

    def remote(src, dst, sends, recvs, i, to):
        return pltpu.make_async_remote_copy(
            src_ref=src, dst_ref=dst, send_sem=sends.at[i], recv_sem=recvs.at[i], device_id=to, device_id_type=MESH
        )

    owns, zs, xs = (kr_ref, qr_ref), (kb, qb), (kx, qx)
    halves = [pl.ds(0, HALF), pl.ds(HALF, HALF)]
    pieces = [pl.ds(h * (A // PIECES), A // PIECES) for h in range(PIECES)]

    def z_copy(n, step, h, way):
        at = step if way == 0 else (8 - step) % 8
        to_at = at + 1 if way == 0 else (at + 7) % 8
        src = (owns[n] if step == 0 else zs[n].at[0, at]).at[pieces[h]]
        dst = (xs[n].at[4] if step == 3 else zs[n].at[0, to_at]).at[pieces[h]]
        return remote(src, dst, z_send, z_recv, ((n * 4 + step) * PIECES + h) * 2 + way, left if way == 0 else right)

    def x_copy(n, t, kind):
        base = owns[n] if t == 0 else xs[n].at[4]
        one, two, three = (xs[n].at[t * 4 + j] for j in (1, 2, 3))
        src, dst, to = (
            (base.at[halves[0]], three.at[halves[0]], xr),
            (base.at[halves[0]], one.at[halves[0]], xl),
            (base.at[halves[1]], three.at[halves[1]], xr),
            (base.at[halves[1]], one.at[halves[1]], xl),
            (three.at[halves[0]], two.at[halves[0]], xr),
            (one.at[halves[1]], two.at[halves[1]], xl),
        )[kind]
        return remote(src, dst, x_send, x_recv, (n * 2 + t) * 6 + kind, to)

    def c_copy(n, r):
        src = owns[n] if r == 0 else zs[n].at[0, r]
        return remote(src, zs[n].at[1, r], c_send, c_recv, n * 8 + r, sibling)

    def y_copy(n, m, d):
        src, dst = ((sk, ans), (sq, qs))[n]
        rows = pl.ds(d * B, B)
        to = across[4 - d] if n == 0 else across[d]
        return remote(src.at[m, rows], dst.at[m, rows], y_send, y_recv, (n * 8 + m) * 4 + d, to)

    def list_copies():
        out = [remote(want_ref.at[d], want_in.at[d], l_send, l_recv, d, across[d]) for d in range(1, 4)]
        for e, f in mates:
            src, dst = table_ref.at[((zl + e) % 4) * 2 + f], table_in.at[zl * 2 + f]
            out.append(remote(src, dst, l_send, l_recv, 4 + e * 2 + f, sky_peer(0, e, f)))
        return out

    def log_copy(t, j):
        return remote(log_row, log_in.at[t * 4 + j], t_send, t_recv, t * 4 + j, loop_peer(t, j))

    def hr_copy(d, e, f):
        src = hr.at[(((zl + e) % 4) * 2 + f) * 4 + d]
        dst = hr_in.at[(zl * 2 + f) * 4 + d]
        return remote(src, dst, t_send, t_recv, 8 + (d * 4 + e) * 2 + f, sky_peer(d, e, f))

    def in_run(r):
        return zl + r <= 3 if r < 4 else zl + r >= 8

    def reaches(step, way):
        src = (zl + step) % 4 if way == 0 else (zl + 8 - step) % 4
        far = src >= 2 if way == 0 else src < 2
        return jnp.where(far, 4, src if way == 0 else 3 - src)

    def z_each(n, step, h, fn):
        for way in range(2):

            @pl.when(reaches(step, way) > step)
            def _(way=way):
                fn(z_copy(n, step, h, way))

    def z_start(n):
        for h in range(PIECES):
            z_each(n, 0, h, lambda copy: copy.start())

    def z_pass(n, step, h):
        for way in range(2):
            hops = reaches(step + 1, way)

            @pl.when(hops > step)
            def _(way=way):
                z_copy(n, step, h, way).wait_recv()

            if step < 3:

                @pl.when(hops > step + 1)
                def _(way=way):
                    z_copy(n, step + 1, h, way).start()

    def sib(n, step, fn):
        for r in (step + 1, 7 - step):

            @pl.when(in_run(r))
            def _(r=r):
                fn(c_copy(n, r))

    def hop(step, fn):
        def one(i, unused):
            r = jnp.where(i < 2, step + 1, 7 - step)
            zz = jnp.where(i < 2, zl + step + 1, zl - step - 1)

            @pl.when((zz >= 0) & (zz <= 3))
            def _():
                fn(r, zz * 2 + i % 2, i % 2)

            return unused

        lax.fori_loop(0, 4, one, 0)

    lane_f = lax.broadcasted_iota(I32, (A, A), 1).astype(F32)
    row_f = lax.broadcasted_iota(I32, (A, A), 0).astype(F32)

    def dense_query(block, own):
        s = nt(qr_ref[...], block[...])
        e = jnp.exp(SCALE * s)
        if own:
            same = lane_f == row_f
            own_s[...] = SCALE * jnp.sum(fold(jnp.where(same, s, 0.0)), axis=1, keepdims=True)
            sums[...] = fold(e)
            acc[...] = nn(jnp.where(same, 0.0, e).astype(BF16), block[...])
        else:
            sums[...] += fold(e)
            acc[...] += nn(e.astype(BF16), block[...])

    def dense_key(block, logs, own):
        s = nt(kr_ref[...], block[...])
        e = jnp.exp(SCALE * s - logs)
        if own:
            e = jnp.where(lane_f == row_f, 0.0, e)
            acck[...] = nn(e.astype(BF16), block[...]) + coef[...] * block[...].astype(F32)
        else:
            acck[...] += nn(e.astype(BF16), block[...])

    def pick(n, m, block):
        col = (kcol, qcol)[n]
        chosen = jnp.where(spread(col[m]) == lane_f, 1.0, 0.0).astype(BF16)
        rows = nn(chosen, block[...]).astype(BF16)
        ((sk, sq)[n])[m] = rows
        ((ans, qs)[n])[m, 0:B, :] = rows[0:B]

    def send_y(n, m):
        for d in range(1, 4):
            y_copy(n, m, d).start()

    def wait_y(n, m):
        for d in range(1, 4):
            y_copy(n, m, d).wait_recv()

    def pick_hop(n, step):
        sib(n, step, lambda copy: copy.wait_recv())
        hop(step, lambda r, m, g: pick(n, m, zs[n].at[g, r]))
        hop(step, lambda r, m, g: send_y(n, m))

    def logits(m):
        wait_y(0, m)
        scores = nt(qr_ref[...], ans[m])
        match = row_f == table_ref[m]
        masked = jnp.where(match, scores, 0.0)
        t = SCALE * jnp.sum(masked, axis=0, keepdims=True)
        tval[m] = t
        tsum[...] += fold(masked)
        tacc[...] += fold(jnp.where(match, jnp.exp(t), 0.0))

    def weights(m):
        match = row_f == table_ref[m]
        w = jnp.where(match, jnp.exp(tval[m]) * spread(share[...]) - spread(inverse[...]), 0.0)
        acc[...] += nn(w.astype(BF16), ans[m])
        h = jnp.sum(w, axis=0, keepdims=True)
        for d in range(4):
            hr[m * 4 + d, 1:2, :] = h[:, d * B : (d + 1) * B]

    def scatter(m):
        wait_y(1, m)
        rows = jnp.concatenate([hr_in[m * 4 + d, 0:1, :] for d in range(4)], axis=1)
        h = jnp.concatenate([hr_in[m * 4 + d, 1:2, :] for d in range(4)], axis=1)
        w = jnp.where(row_f == rows, h, 0.0)
        acck[...] += nn(w.astype(BF16), qs[m])

    def own_pair(fn):
        def one(g, unused):
            fn(zl * 2 + g)
            return unused

        lax.fori_loop(0, 2, one, 0)

    def z_step(n, step):
        for h in range(PIECES):
            z_pass(n, step, h)
            if step == 3 and h == PIECES // 2 - 1:
                x_start(n, 1, 0)
        if step < 3:
            sib(n, step, lambda copy: copy.start())
        else:
            x_start(n, 1, 1)

    def x_start(n, t, h):
        for kind in range(2):
            x_copy(n, t, h * 2 + kind).start()

    def x_turn(n, t):
        x_copy(n, t, 0).wait_recv()
        x_copy(n, t, 4).start()
        x_copy(n, t, 3).wait_recv()
        x_copy(n, t, 5).start()
        for kind in (1, 2):
            x_copy(n, t, kind).wait_recv()

    def x_end(n, t):
        for kind in (4, 5):
            x_copy(n, t, kind).wait_recv()

    def sides(t, fn):
        def one(i, unused):
            fn(t * 4 + 1 + 2 * i)
            return unused

        lax.fori_loop(0, 2, one, 0)

    pick(1, zl * 2, qr_ref)
    pl.semaphore_wait(barrier, len(greeted))
    lists = list_copies()
    for copy in lists:
        copy.start()
    send_y(1, zl * 2)
    z_start(0)
    c_copy(1, 0).start()
    c_copy(0, 0).start()
    x_start(0, 0, 0)
    x_start(0, 0, 1)
    own_lists = [
        pltpu.make_async_copy(want_ref.at[0], want_in.at[0], local.at[0]),
        pltpu.make_async_copy(table_ref.at[zl * 2], table_in.at[zl * 2], local.at[1]),
    ]
    for copy in own_lists:
        copy.start()
    dense_query(kr_ref, True)
    for copy in lists:
        copy.wait_recv()
    for copy in own_lists:
        copy.wait()
    def columns(listed, cols):
        turned = jnp.transpose(listed)
        for m in range(8):
            cols[m] = jnp.broadcast_to(turned[:, m : m + 1], (A, 128))

    columns(jnp.concatenate([table_in[m] for m in range(8)], axis=0), qcol)
    c_copy(1, 0).wait_recv()
    pick(1, zl * 2 + 1, qb.at[1, 0])
    send_y(1, zl * 2 + 1)
    columns(jnp.concatenate([want_in[d] for d in range(4)], axis=1), kcol)
    pick(0, zl * 2, kr_ref)
    c_copy(0, 0).wait_recv()
    pick(0, zl * 2 + 1, kb.at[1, 0])
    for g in range(2):
        send_y(0, zl * 2 + g)
    z_step(0, 0)
    x_turn(0, 0)
    x_start(1, 0, 0)
    x_start(1, 0, 1)
    sides(0, lambda b: dense_query(kx.at[b], False))
    pick_hop(0, 0)
    z_step(0, 1)
    z_start(1)
    x_end(0, 0)
    dense_query(kx.at[2], False)
    pick_hop(0, 1)
    x_turn(1, 0)
    own_pair(logits)
    z_step(0, 2)
    pick_hop(0, 2)
    z_step(1, 0)
    z_step(0, 3)
    dense_query(kx.at[4], False)
    pick_hop(1, 0)
    z_step(1, 1)
    hop(0, lambda r, m, g: logits(m))
    x_turn(0, 1)
    sides(1, lambda b: dense_query(kx.at[b], False))
    pick_hop(1, 1)
    z_step(1, 2)
    x_end(0, 1)
    dense_query(kx.at[6], False)
    hop(1, lambda r, m, g: logits(m))
    pick_hop(1, 2)
    hop(2, lambda r, m, g: logits(m))

    total = jnp.sum(sums[...] + tacc[...], axis=1, keepdims=True)
    log_total = jnp.log(total)
    inv = inverse[:, 0:1]
    loss = log_total - inv * (own_s[...] + SCALE * jnp.sum(tsum[...], axis=1, keepdims=True))
    lane = lax.broadcasted_iota(I32, (A, 128), 1)
    turned = jnp.transpose(jnp.where(lane == 0, loss, log_total))
    loss_ref[...] = turned[0:1, :]
    log_row[...] = turned[1:2, :]
    mine = (jnp.exp(own_s[...] - log_total) - inv).astype(BF16).astype(F32)
    coef[...] = mine
    share[...] = jnp.broadcast_to(1.0 / total, (A, 128))
    acc[...] = acc[...] * (1.0 / total) + mine * kr_ref[...].astype(F32)
    weights(0)
    for t, j in loops:
        log_copy(t, j).start()

    def more(m, unused):
        weights(m)
        return unused

    lax.fori_loop(1, 4, more, 0)
    z_step(1, 3)
    lax.fori_loop(4, 8, more, 0)
    for sky in skies:
        hr_copy(*sky).start()
    own_hr = pltpu.make_async_copy(hr.at[(zl * 2) * 4], hr_in.at[(zl * 2) * 4], local.at[2])
    own_hr.start()
    dense_key(qr_ref, log_row[...], True)
    x_end(1, 0)
    for t, j in loops:
        log_copy(t, j).wait_recv()

    def near(j, unused):
        dense_key(qx.at[j], log_in[j], False)
        return unused

    lax.fori_loop(1, 5, near, 0)
    x_turn(1, 1)
    own_hr.wait()
    for sky in skies:
        hr_copy(*sky).wait_recv()
    own_pair(scatter)
    hop(0, lambda r, m, g: scatter(m))
    sides(1, lambda b: dense_key(qx.at[b], log_in[b], False))
    x_end(1, 1)
    dense_key(qx.at[6], log_in[6], False)
    hop(1, lambda r, m, g: scatter(m))
    hop(2, lambda r, m, g: scatter(m))

    for copy in lists:
        copy.wait_send()
    for n in range(2):
        for step in range(4):
            for h in range(PIECES):
                z_each(n, step, h, lambda copy: copy.wait_send())
        for t in range(2):
            for kind in range(6):
                x_copy(n, t, kind).wait_send()
        c_copy(n, 0).wait_send()
        for step in range(3):
            sib(n, step, lambda copy: copy.wait_send())
        for m in range(8):
            for d in range(1, 4):
                y_copy(n, m, d).wait_send()
    for t, j in loops:
        log_copy(t, j).wait_send()
    for sky in skies:
        hr_copy(*sky).wait_send()


def everything(queries, keys, rel, row, count):
    shape = jax.ShapeDtypeStruct
    vm = pltpu.VMEM
    dma = pltpu.SemaphoreType.DMA
    eight = vm((8, A, D), BF16)
    both = vm((2, 8, A, D), BF16)
    column = vm((A, 1), F32)
    narrow = vm((A, 128), F32)
    return pl.pallas_call(
        total_kernel,
        name="everything",
        out_shape=(shape((1, A), F32), shape((A, D), F32), shape((A, D), F32)),
        in_specs=[VMEM] * 5,
        out_specs=(VMEM,) * 3,
        scratch_shapes=[vm((A, D), BF16)] * 2
        + [vm((4, 8, B), F32), vm((8, 1, A), F32)]
        + [both, both]
        + [eight] * 6
        + [vm((8, A, 128), F32)] * 2
        + [vm((4, 8, B), F32), vm((8, 1, A), F32)]
        + [narrow] * 3
        + [column, narrow, narrow, column]
        + [vm((8, 1, A), F32), vm((1, A), F32), vm((8, 1, A), F32)]
        + [vm((32, 2, B), F32)] * 2
        + [dma((64,))] * 2
        + [dma((24,))] * 2
        + [dma((16,))] * 2
        + [dma((12,))] * 2
        + [dma((64,))] * 2
        + [dma((40,))] * 2
        + [dma((3,))],
        compiler_params=params(collective_id=0, has_side_effects=True),
    )(queries, keys, rel, row, count)


def finish_kernel(q_ref, k_ref, gq_ref, gk_ref, row_ref, out_q, out_k, out_row):
    for src, total, out in ((q_ref, gq_ref, out_q), (k_ref, gk_ref, out_k)):
        wide = src[...].astype(F32)
        norm = jnp.sqrt(jnp.sum(wide * wide, axis=1, keepdims=True) + EPS)
        unit = wide / norm
        g = SCALE * total[...]
        out[...] = (g - unit * jnp.sum(unit * g, axis=1, keepdims=True)) / norm
    out_row[...] = row_ref[...]


def finish(queries, keys, gq, gk, row):
    shape = jax.ShapeDtypeStruct
    block = pl.BlockSpec((256, D), lambda i: (i, 0))
    lanes = pl.BlockSpec((1, 256), lambda i: (0, i))
    return pl.pallas_call(
        finish_kernel,
        name="finish",
        grid=(A // 256,),
        out_shape=(shape((A, D), F32), shape((A, D), F32), shape((1, A), F32)),
        in_specs=[block] * 4 + [lanes],
        out_specs=(block, block, lanes),
        compiler_params=params(),
    )(queries, keys, gq, gk, row)


def shards(queries, keys, partner_owner, partner_row, partner_count):
    row, gq, gk = everything(queries, keys, partner_owner.T, partner_row.T, partner_count)
    grad_q, grad_k, row = finish(queries, keys, gq, gk, row)
    return row.reshape(A), grad_q, grad_k


def solution(mesh):
    rows, flat = P(("sky", "loop"), None), P(("sky", "loop"))
    return jax.shard_map(
        shards,
        mesh=mesh,
        in_specs=(rows, rows, rows, rows, flat),
        out_specs=(flat, rows, rows),
        check_vma=False,
    )
```

```python
import functools

import jax
import jax.numpy as jnp
from jax import lax
from jax.experimental import pallas as pl
from jax.experimental.pallas import tpu as pltpu
from jax.sharding import PartitionSpec as P

SCALE = 10.0
EPS = 1e-06
A = 768
D = 256
B = 192
HALF = A // 2
PIECES = 4
MESH = pl.DeviceIdType.MESH
F32 = jnp.float32
BF16 = jnp.bfloat16
I32 = jnp.int32
VMEM = pl.BlockSpec(memory_space=pltpu.VMEM)
ANY = pl.BlockSpec(memory_space=pl.ANY)


def params(**more):
    return pltpu.CompilerParams(vmem_limit_bytes=60000 * 1024, **more)


def nt(a, b):
    return lax.dot_general(a, b, (((1,), (1,)), ((), ())), preferred_element_type=F32)


def nn(a, b):
    return jnp.dot(a, b, preferred_element_type=F32)


def place():
    sky, loop = lax.axis_index("sky"), lax.axis_index("loop")
    return sky // 8, (sky // 2) % 4, sky % 2, loop // 2, loop % 2


def device(y, z, c, x):
    return ((y * 4 + z % 4) * 2 + c, x * 2 + z // 4)


def unit_block(src, dst):
    wide = src[...].astype(F32)
    norm = jnp.sqrt(jnp.sum(wide * wide, axis=1, keepdims=True) + EPS)
    dst[...] = (wide / norm).astype(BF16)


def slot_lists(rel, row_ref, want_ref, table_ref):
    sky = lax.broadcasted_iota(I32, (32, A), 0)
    hits = [rel[p : p + 1, :] == sky for p in range(4)]
    hit = sum(jnp.where(h, 1.0, 0.0) for h in hits).astype(BF16)
    below = lax.broadcasted_iota(I32, (A, A), 0) < lax.broadcasted_iota(I32, (A, A), 1)
    rank = nn(hit, jnp.where(below, 1.0, 0.0).astype(BF16))
    anchor = lax.broadcasted_iota(I32, (1, A), 1) + 1
    lists = jnp.zeros((128, B), F32)
    slot = lax.broadcasted_iota(I32, (B, A), 0).astype(F32)
    for p in range(4):
        mine = jnp.sum(jnp.where(hits[p], rank, 0.0), axis=0, keepdims=True)
        chosen = jnp.where(slot == mine, 1.0, 0.0).astype(BF16)
        row = row_ref[p : p + 1, :] + 1
        parts = [anchor % 256, anchor // 256, row % 256, row // 256]
        values = jnp.concatenate(
            [jnp.where(hits[p], part.astype(F32), 0.0) for part in parts], axis=0
        ).astype(BF16)
        lists = lists + nt(values, chosen)
    anchors = lists[0:32] + 256.0 * lists[32:64] - 1.0
    wanted = lists[64:96] + 256.0 * lists[96:128] - 1.0
    for d in range(4):
        want_ref[d] = wanted[d * 8 : d * 8 + 8]
    table = jnp.concatenate([anchors[d * 8 : d * 8 + 8] for d in range(4)], axis=1)
    for m in range(8):
        table_ref[m] = table[m : m + 1]


def fold(wide):
    out = wide[:, 0:128]
    for i in range(1, wide.shape[1] // 128):
        out = out + wide[:, i * 128 : (i + 1) * 128]
    return out


def spread(narrow):
    return jnp.concatenate([narrow] * (A // 128), axis=1)


def total_kernel(
    q_ref, k_ref, owner_ref, row_ref, count_ref,
    loss_ref, acc, acck,
    qr_ref, kr_ref, want_ref, table_ref,
    kb, qb, kx, qx, sk, sq, ans, qs, kcol, qcol, want_in, table_in,
    sums, tacc, tsum, own_s, share, inverse, coef, tval, log_row, log_in, hr, hr_in,
    z_send, z_recv, x_send, x_recv, c_send, c_recv, l_send, l_recv, y_send, y_recv, t_send, t_recv, local,
):
    y, zl, c, x, zh = place()
    z = zh * 4 + zl
    left, right = device(y, (z + 7) % 8, c, x), device(y, (z + 1) % 8, c, x)
    xl, xr = device(y, z, c, (x + 3) % 4), device(y, z, c, (x + 1) % 4)
    sibling = device(y, z, 1 - c, x)
    across = [device((y + d) % 4, z, c, x) for d in range(4)]
    mates = [(e, f) for e in range(4) for f in range(2) if (e, f) != (0, 0)]
    loops = [(t, j) for t in range(2) for j in range(4) if (t, j) != (0, 0)]
    skies = [(d, e, f) for d in range(4) for e in range(4) for f in range(2) if (d, e, f) != (0, 0, 0)]

    def loop_peer(t, j):
        return device(y, (z + 4 * t) % 8, c, (x + 4 - j) % 4)

    def sky_peer(d, e, f):
        return device((y + d) % 4, zh * 4 + (zl + e) % 4, (c + f) % 2, x)

    barrier = pltpu.get_barrier_semaphore()
    greeted = [left, right, xl, xr] + across[1:] + [sky_peer(0, *p) for p in mates]
    for other in greeted:
        pl.semaphore_signal(barrier, inc=1, device_id=other, device_id_type=MESH)
    unit_block(k_ref, kr_ref)
    unit_block(q_ref, qr_ref)
    owner, count = owner_ref[...], count_ref[...].reshape(1, A)
    rel = ((owner // 8 - y + 4) % 4) * 8 + owner % 8 // 2 * 2 + (owner + c) % 2
    rel = jnp.where(lax.broadcasted_iota(I32, (4, A), 0) < count, rel, -1)
    slot_lists(rel, row_ref, want_ref, table_ref)
    pair = jnp.concatenate([count.astype(F32), table_ref[zl * 2]] + [jnp.zeros((6, A), F32)], axis=0)
    turned = jnp.transpose(pair)
    inverse[...] = jnp.broadcast_to(1.0 / (1.0 + turned[:, 0:1]), (A, 128))
    qcol[zl * 2] = jnp.broadcast_to(turned[:, 1:2], (A, 128))
    for d in range(4):
        for m in range(8):
            hr[m * 4 + d, 0:1, :] = want_ref[d, m : m + 1, :]
    tacc[...] = jnp.zeros_like(tacc)
    tsum[...] = jnp.zeros_like(tsum)

    def remote(src, dst, sends, recvs, i, to):
        return pltpu.make_async_remote_copy(
            src_ref=src, dst_ref=dst, send_sem=sends.at[i], recv_sem=recvs.at[i], device_id=to, device_id_type=MESH
        )

    owns, zs, xs = (kr_ref, qr_ref), (kb, qb), (kx, qx)
    halves = [pl.ds(0, HALF), pl.ds(HALF, HALF)]
    pieces = [pl.ds(h * (A // PIECES), A // PIECES) for h in range(PIECES)]

    def z_copy(n, step, h, way):
        at = step if way == 0 else (8 - step) % 8
        to_at = at + 1 if way == 0 else (at + 7) % 8
        src = (owns[n] if step == 0 else zs[n].at[0, at]).at[pieces[h]]
        dst = (xs[n].at[4] if step == 3 else zs[n].at[0, to_at]).at[pieces[h]]
        return remote(src, dst, z_send, z_recv, ((n * 4 + step) * PIECES + h) * 2 + way, left if way == 0 else right)

    def x_copy(n, t, kind):
        base = owns[n] if t == 0 else xs[n].at[4]
        one, two, three = (xs[n].at[t * 4 + j] for j in (1, 2, 3))
        src, dst, to = (
            (base.at[halves[0]], three.at[halves[0]], xr),
            (base.at[halves[0]], one.at[halves[0]], xl),
            (base.at[halves[1]], three.at[halves[1]], xr),
            (base.at[halves[1]], one.at[halves[1]], xl),
            (three.at[halves[0]], two.at[halves[0]], xr),
            (one.at[halves[1]], two.at[halves[1]], xl),
        )[kind]
        return remote(src, dst, x_send, x_recv, (n * 2 + t) * 6 + kind, to)

    def c_copy(n, r):
        src = owns[n] if r == 0 else zs[n].at[0, r]
        return remote(src, zs[n].at[1, r], c_send, c_recv, n * 8 + r, sibling)

    def y_copy(n, m, d):
        src, dst = ((sk, ans), (sq, qs))[n]
        rows = pl.ds(d * B, B)
        to = across[4 - d] if n == 0 else across[d]
        return remote(src.at[m, rows], dst.at[m, rows], y_send, y_recv, (n * 8 + m) * 4 + d, to)

    def list_copies():
        out = [remote(want_ref.at[d], want_in.at[d], l_send, l_recv, d, across[d]) for d in range(1, 4)]
        for e, f in mates:
            src, dst = table_ref.at[((zl + e) % 4) * 2 + f], table_in.at[zl * 2 + f]
            out.append(remote(src, dst, l_send, l_recv, 4 + e * 2 + f, sky_peer(0, e, f)))
        return out

    def log_copy(t, j):
        return remote(log_row, log_in.at[t * 4 + j], t_send, t_recv, t * 4 + j, loop_peer(t, j))

    def hr_copy(d, e, f):
        src = hr.at[(((zl + e) % 4) * 2 + f) * 4 + d]
        dst = hr_in.at[(zl * 2 + f) * 4 + d]
        return remote(src, dst, t_send, t_recv, 8 + (d * 4 + e) * 2 + f, sky_peer(d, e, f))

    def in_run(r):
        return zl + r <= 3 if r < 4 else zl + r >= 8

    def reaches(step, way):
        src = (zl + step) % 4 if way == 0 else (zl + 8 - step) % 4
        far = src >= 2 if way == 0 else src < 2
        return jnp.where(far, 4, src if way == 0 else 3 - src)

    def z_each(n, step, h, fn):
        for way in range(2):

            @pl.when(reaches(step, way) > step)
            def _(way=way):
                fn(z_copy(n, step, h, way))

    def z_start(n):
        for h in range(PIECES):
            z_each(n, 0, h, lambda copy: copy.start())

    def z_pass(n, step, h):
        for way in range(2):
            hops = reaches(step + 1, way)

            @pl.when(hops > step)
            def _(way=way):
                z_copy(n, step, h, way).wait_recv()

            if step < 3:

                @pl.when(hops > step + 1)
                def _(way=way):
                    z_copy(n, step + 1, h, way).start()

    def sib(n, step, fn):
        for r in (step + 1, 7 - step):

            @pl.when(in_run(r))
            def _(r=r):
                fn(c_copy(n, r))

    def hop(step, fn):
        def one(i, unused):
            r = jnp.where(i < 2, step + 1, 7 - step)
            zz = jnp.where(i < 2, zl + step + 1, zl - step - 1)

            @pl.when((zz >= 0) & (zz <= 3))
            def _():
                fn(r, zz * 2 + i % 2, i % 2)

            return unused

        lax.fori_loop(0, 4, one, 0)

    lane_f = lax.broadcasted_iota(I32, (A, A), 1).astype(F32)
    row_f = lax.broadcasted_iota(I32, (A, A), 0).astype(F32)

    def dense_query(block, own):
        s = nt(qr_ref[...], block[...])
        e = jnp.exp(SCALE * s)
        if own:
            same = lane_f == row_f
            own_s[...] = SCALE * jnp.sum(fold(jnp.where(same, s, 0.0)), axis=1, keepdims=True)
            sums[...] = fold(e)
            acc[...] = nn(jnp.where(same, 0.0, e).astype(BF16), block[...])
        else:
            sums[...] += fold(e)
            acc[...] += nn(e.astype(BF16), block[...])

    def dense_key(block, logs, own):
        s = nt(kr_ref[...], block[...])
        e = jnp.exp(SCALE * s - logs)
        if own:
            e = jnp.where(lane_f == row_f, 0.0, e)
            acck[...] = nn(e.astype(BF16), block[...]) + coef[...] * block[...].astype(F32)
        else:
            acck[...] += nn(e.astype(BF16), block[...])

    def pick(n, m, block):
        col = (kcol, qcol)[n]
        chosen = jnp.where(spread(col[m]) == lane_f, 1.0, 0.0).astype(BF16)
        rows = nn(chosen, block[...]).astype(BF16)
        ((sk, sq)[n])[m] = rows
        ((ans, qs)[n])[m, 0:B, :] = rows[0:B]

    def send_y(n, m):
        for d in range(1, 4):
            y_copy(n, m, d).start()

    def wait_y(n, m):
        for d in range(1, 4):
            y_copy(n, m, d).wait_recv()

    def pick_hop(n, step):
        sib(n, step, lambda copy: copy.wait_recv())
        hop(step, lambda r, m, g: pick(n, m, zs[n].at[g, r]))
        hop(step, lambda r, m, g: send_y(n, m))

    def logits(m):
        wait_y(0, m)
        scores = nt(qr_ref[...], ans[m])
        match = row_f == table_ref[m]
        masked = jnp.where(match, scores, 0.0)
        t = SCALE * jnp.sum(masked, axis=0, keepdims=True)
        tval[m] = t
        tsum[...] += fold(masked)
        tacc[...] += fold(jnp.where(match, jnp.exp(t), 0.0))

    def weights(m):
        match = row_f == table_ref[m]
        w = jnp.where(match, jnp.exp(tval[m]) * spread(share[...]) - spread(inverse[...]), 0.0)
        acc[...] += nn(w.astype(BF16), ans[m])
        h = jnp.sum(w, axis=0, keepdims=True)
        for d in range(4):
            hr[m * 4 + d, 1:2, :] = h[:, d * B : (d + 1) * B]

    def scatter(m):
        wait_y(1, m)
        rows = jnp.concatenate([hr_in[m * 4 + d, 0:1, :] for d in range(4)], axis=1)
        h = jnp.concatenate([hr_in[m * 4 + d, 1:2, :] for d in range(4)], axis=1)
        w = jnp.where(row_f == rows, h, 0.0)
        acck[...] += nn(w.astype(BF16), qs[m])

    def own_pair(fn):
        def one(g, unused):
            fn(zl * 2 + g)
            return unused

        lax.fori_loop(0, 2, one, 0)

    def z_step(n, step):
        for h in range(PIECES):
            z_pass(n, step, h)
            if step == 3 and h == PIECES // 2 - 1:
                x_start(n, 1, 0)
        if step < 3:
            sib(n, step, lambda copy: copy.start())
        else:
            x_start(n, 1, 1)

    def x_start(n, t, h):
        for kind in range(2):
            x_copy(n, t, h * 2 + kind).start()

    def x_turn(n, t):
        x_copy(n, t, 0).wait_recv()
        x_copy(n, t, 4).start()
        x_copy(n, t, 3).wait_recv()
        x_copy(n, t, 5).start()
        for kind in (1, 2):
            x_copy(n, t, kind).wait_recv()

    def x_end(n, t):
        for kind in (4, 5):
            x_copy(n, t, kind).wait_recv()

    def sides(t, fn):
        def one(i, unused):
            fn(t * 4 + 1 + 2 * i)
            return unused

        lax.fori_loop(0, 2, one, 0)

    pick(1, zl * 2, qr_ref)
    pl.semaphore_wait(barrier, len(greeted))
    lists = list_copies()
    for copy in lists:
        copy.start()
    send_y(1, zl * 2)
    z_start(0)
    c_copy(1, 0).start()
    c_copy(0, 0).start()
    x_start(0, 0, 0)
    x_start(0, 0, 1)
    own_lists = [
        pltpu.make_async_copy(want_ref.at[0], want_in.at[0], local.at[0]),
        pltpu.make_async_copy(table_ref.at[zl * 2], table_in.at[zl * 2], local.at[1]),
    ]
    for copy in own_lists:
        copy.start()
    dense_query(kr_ref, True)
    for copy in lists:
        copy.wait_recv()
    for copy in own_lists:
        copy.wait()
    def columns(listed, cols):
        turned = jnp.transpose(listed)
        for m in range(8):
            cols[m] = jnp.broadcast_to(turned[:, m : m + 1], (A, 128))

    columns(jnp.concatenate([table_in[m] for m in range(8)], axis=0), qcol)
    c_copy(1, 0).wait_recv()
    pick(1, zl * 2 + 1, qb.at[1, 0])
    send_y(1, zl * 2 + 1)
    columns(jnp.concatenate([want_in[d] for d in range(4)], axis=1), kcol)
    pick(0, zl * 2, kr_ref)
    c_copy(0, 0).wait_recv()
    pick(0, zl * 2 + 1, kb.at[1, 0])
    for g in range(2):
        send_y(0, zl * 2 + g)
    z_step(0, 0)
    x_turn(0, 0)
    x_start(1, 0, 0)
    x_start(1, 0, 1)
    sides(0, lambda b: dense_query(kx.at[b], False))
    pick_hop(0, 0)
    z_step(0, 1)
    z_start(1)
    x_end(0, 0)
    dense_query(kx.at[2], False)
    pick_hop(0, 1)
    x_turn(1, 0)
    own_pair(logits)
    z_step(0, 2)
    pick_hop(0, 2)
    z_step(1, 0)
    z_step(0, 3)
    dense_query(kx.at[4], False)
    pick_hop(1, 0)
    z_step(1, 1)
    hop(0, lambda r, m, g: logits(m))
    x_turn(0, 1)
    sides(1, lambda b: dense_query(kx.at[b], False))
    pick_hop(1, 1)
    z_step(1, 2)
    x_end(0, 1)
    dense_query(kx.at[6], False)
    hop(1, lambda r, m, g: logits(m))
    pick_hop(1, 2)
    hop(2, lambda r, m, g: logits(m))

    total = jnp.sum(sums[...] + tacc[...], axis=1, keepdims=True)
    log_total = jnp.log(total)
    inv = inverse[:, 0:1]
    loss = log_total - inv * (own_s[...] + SCALE * jnp.sum(tsum[...], axis=1, keepdims=True))
    lane = lax.broadcasted_iota(I32, (A, 128), 1)
    turned = jnp.transpose(jnp.where(lane == 0, loss, log_total))
    loss_ref[...] = turned[0:1, :]
    log_row[...] = turned[1:2, :]
    mine = (jnp.exp(own_s[...] - log_total) - inv).astype(BF16).astype(F32)
    coef[...] = mine
    share[...] = jnp.broadcast_to(1.0 / total, (A, 128))
    acc[...] = acc[...] * (1.0 / total) + mine * kr_ref[...].astype(F32)
    weights(0)
    for t, j in loops:
        log_copy(t, j).start()

    def more(m, unused):
        weights(m)
        return unused

    lax.fori_loop(1, 4, more, 0)
    z_step(1, 3)
    lax.fori_loop(4, 8, more, 0)
    for sky in skies:
        hr_copy(*sky).start()
    own_hr = pltpu.make_async_copy(hr.at[(zl * 2) * 4], hr_in.at[(zl * 2) * 4], local.at[2])
    own_hr.start()
    dense_key(qr_ref, log_row[...], True)
    x_end(1, 0)
    for t, j in loops:
        log_copy(t, j).wait_recv()

    def near(j, unused):
        dense_key(qx.at[j], log_in[j], False)
        return unused

    lax.fori_loop(1, 5, near, 0)
    x_turn(1, 1)
    own_hr.wait()
    for sky in skies:
        hr_copy(*sky).wait_recv()
    own_pair(scatter)
    hop(0, lambda r, m, g: scatter(m))
    sides(1, lambda b: dense_key(qx.at[b], log_in[b], False))
    hop(1, lambda r, m, g: scatter(m))
    hop(2, lambda r, m, g: scatter(m))
    x_end(1, 1)
    dense_key(qx.at[6], log_in[6], False)

    for copy in lists:
        copy.wait_send()
    for n in range(2):
        for step in range(4):
            for h in range(PIECES):
                z_each(n, step, h, lambda copy: copy.wait_send())
        for t in range(2):
            for kind in range(6):
                x_copy(n, t, kind).wait_send()
        c_copy(n, 0).wait_send()
        for step in range(3):
            sib(n, step, lambda copy: copy.wait_send())
        for m in range(8):
            for d in range(1, 4):
                y_copy(n, m, d).wait_send()
    for t, j in loops:
        log_copy(t, j).wait_send()
    for sky in skies:
        hr_copy(*sky).wait_send()


def everything(queries, keys, rel, row, count):
    shape = jax.ShapeDtypeStruct
    vm = pltpu.VMEM
    dma = pltpu.SemaphoreType.DMA
    eight = vm((8, A, D), BF16)
    both = vm((2, 8, A, D), BF16)
    column = vm((A, 1), F32)
    narrow = vm((A, 128), F32)
    return pl.pallas_call(
        total_kernel,
        name="everything",
        out_shape=(shape((1, A), F32), shape((A, D), F32), shape((A, D), F32)),
        in_specs=[VMEM] * 5,
        out_specs=(VMEM,) * 3,
        scratch_shapes=[vm((A, D), BF16)] * 2
        + [vm((4, 8, B), F32), vm((8, 1, A), F32)]
        + [both, both]
        + [eight] * 6
        + [vm((8, A, 128), F32)] * 2
        + [vm((4, 8, B), F32), vm((8, 1, A), F32)]
        + [narrow] * 3
        + [column, narrow, narrow, column]
        + [vm((8, 1, A), F32), vm((1, A), F32), vm((8, 1, A), F32)]
        + [vm((32, 2, B), F32)] * 2
        + [dma((64,))] * 2
        + [dma((24,))] * 2
        + [dma((16,))] * 2
        + [dma((12,))] * 2
        + [dma((64,))] * 2
        + [dma((40,))] * 2
        + [dma((3,))],
        compiler_params=params(collective_id=0, has_side_effects=True),
    )(queries, keys, rel, row, count)


def finish_kernel(q_ref, k_ref, gq_ref, gk_ref, row_ref, out_q, out_k, out_row):
    for src, total, out in ((q_ref, gq_ref, out_q), (k_ref, gk_ref, out_k)):
        wide = src[...].astype(F32)
        norm = jnp.sqrt(jnp.sum(wide * wide, axis=1, keepdims=True) + EPS)
        unit = wide / norm
        g = SCALE * total[...]
        out[...] = (g - unit * jnp.sum(unit * g, axis=1, keepdims=True)) / norm
    out_row[...] = row_ref[...]


def finish(queries, keys, gq, gk, row):
    shape = jax.ShapeDtypeStruct
    block = pl.BlockSpec((384, D), lambda i: (i, 0))
    lanes = pl.BlockSpec((1, 384), lambda i: (0, i))
    return pl.pallas_call(
        finish_kernel,
        name="finish",
        grid=(A // 384,),
        out_shape=(shape((A, D), F32), shape((A, D), F32), shape((1, A), F32)),
        in_specs=[block] * 4 + [lanes],
        out_specs=(block, block, lanes),
        compiler_params=params(),
    )(queries, keys, gq, gk, row)


def shards(queries, keys, partner_owner, partner_row, partner_count):
    row, gq, gk = everything(queries, keys, partner_owner.T, partner_row.T, partner_count)
    grad_q, grad_k, row = finish(queries, keys, gq, gk, row)
    return row.reshape(A), grad_q, grad_k


def solution(mesh):
    rows, flat = P(("sky", "loop"), None), P(("sky", "loop"))
    return jax.shard_map(
        shards,
        mesh=mesh,
        in_specs=(rows, rows, rows, rows, flat),
        out_specs=(flat, rows, rows),
        check_vma=False,
    )
```
